128 devices in a mesh: rows: 16 (over x, z_hi, core), probe: 8 (over z_lo, y).
Axes of the slice: x: 4, y: 4, z: 4 (z_hi: 2, z_lo: 2; z = z_hi * 2 + z_lo), core: 2. Of those that a mesh axis runs over, the one named last changes fastest.
Arguments:
- responses: bfloat16 [256, 131072], P('probe', 'rows'), may hold values from -6 to 6
- probes: bfloat16 [256, 131072], P('probe', 'rows'), may hold values from -6 to 6
- left_factors: bfloat16 [5, 128, 131072], P(None, None, 'rows'), may hold values from -0.5 to 0.5
- right_factors: bfloat16 [5, 128, 131072], P(None, None, 'rows'), may hold values from -0.09375 to 0.09375
- level_ranks: int32 [5], replicated, may hold values from 32 to 128, as said below
Outputs:
- basis: float32 [256, 131072], P(None, ('rows', 'probe'))
The draws below stay inside these ranges and needn't reach their ends.
Inputs may be any that keep to these rules, and one draw needn't show every extreme that they name: `level_ranks`: some level has rank 128 and some level rank 128 // 4.
All inputs are finite; a program needn't handle non-finite values.
Results may differ from the reference program's by a relative error of at most 0.0047.
Values may be sent and summed in bfloat16 or wider, within the bound.
A program may use at most 128 MiB of HBM per device.

```python
import jax
import jax.numpy as jnp
from jax import lax

PROBES = 256
RANK = 128
COARSE = 5
BLOCKS = 64
ORDER = 131072


def draw_right_factors(key, part):
    depths = jnp.arange(1, COARSE + 1).astype(jnp.float32)
    cluster_rows = jnp.float32(ORDER) / 2.0 ** depths
    scales = 1.0 / jnp.sqrt(cluster_rows)
    values = jax.random.truncated_normal(key, -6.0, 6.0, (COARSE, RANK, ORDER), jnp.float32)
    return (values * scales[:, None, None]).astype(jnp.bfloat16)


def draw_level_ranks(key, part):
    first_key = jax.random.fold_in(key, 11)
    second_key = jax.random.fold_in(key, 12)
    third_key = jax.random.fold_in(key, 13)
    ranks_drawn = jax.random.randint(first_key, (COARSE,), RANK // 4, RANK + 1)
    top_slot = jax.random.randint(second_key, (), 0, COARSE)
    low_slot = (top_slot + 1 + jax.random.randint(third_key, (), 0, COARSE - 1)) % COARSE
    ranks_drawn = ranks_drawn.at[top_slot].set(RANK)
    ranks_drawn = ranks_drawn.at[low_slot].set(RANK // 4)
    return ranks_drawn.astype(jnp.int32)


def shard_levels(own_key, dims, shards, low, largest):
    factor_of = 1.0
    for axis_at, parts in shards:
        heights = jax.random.uniform(jax.random.fold_in(jax.random.fold_in(own_key, 6), axis_at), (parts,), jnp.float32, low / len(shards), largest / len(shards))
        factor_of = factor_of * jnp.repeat(jnp.exp(heights), dims[axis_at] // parts).reshape((-1,) + (1,) * (len(dims) - 1 - axis_at))
    return factor_of


def normal_values(stream_key, dims, scale, bound, cuts=(), held_as=jnp.bfloat16):
    entries = jax.random.normal(stream_key, dims, jnp.float32) * scale
    if len(cuts) > 0:
        entries = shard_levels(stream_key, dims, cuts, -0.22, 0.18) * entries
    return jnp.clip(entries, min=-bound, max=bound).astype(held_as)


def setup_inputs(seed: int = 0) -> dict:
    key_of = jax.random.split(jax.random.key(seed), 6)
    responses = normal_values(key_of[0], (PROBES, ORDER), 1.0, 6.0, ((0, 8), (1, 16)))
    probes = normal_values(key_of[1], (PROBES, ORDER), 1.0, 6.0, ((0, 8), (1, 16)))
    left_factors = normal_values(key_of[2], (COARSE, RANK, ORDER), RANK ** -0.5, 0.5, ((2, 16),))
    right_factors = draw_right_factors(jax.random.fold_in(key_of[5], 71), 0)
    level_ranks = draw_level_ranks(jax.random.fold_in(key_of[5], 71), 0)
    return dict(responses=responses, probes=probes, left_factors=left_factors, right_factors=right_factors, level_ranks=level_ranks)


ridge_share = 0.05

def reference(responses, probes, left_factors, right_factors, level_ranks):
    probe_total, order_rows = responses.shape
    residual = responses.astype(jnp.float32)
    rank_iota = jnp.arange(RANK)
    probe_wide = probes.astype(jnp.float32)
    for level_index in range(COARSE):
        clusters = 2 ** (level_index + 1)
        cluster_rows = order_rows // clusters
        right_part = right_factors[level_index].astype(jnp.float32).reshape(RANK, clusters, cluster_rows)
        probe_part = probe_wide.reshape(probe_total, clusters, cluster_rows)
        coupling = jnp.einsum('kcn,rcn->ckr', right_part, probe_part, precision=lax.Precision.HIGHEST)
        coupling = jnp.where(rank_iota[None, :, None] < level_ranks[level_index], coupling, 0.0)
        sibling = coupling.reshape(clusters // 2, 2, RANK, probe_total)[:, ::-1]
        sibling = sibling.reshape(clusters, RANK, probe_total).astype(jnp.bfloat16)
        left_part = left_factors[level_index].astype(jnp.float32).reshape(RANK, clusters, cluster_rows)
        update = jnp.einsum('ckr,kcn->rcn', sibling.astype(jnp.float32), left_part, precision=lax.Precision.HIGHEST)
        residual = residual - update.reshape(probe_total, order_rows)
    sample = residual.astype(jnp.bfloat16)
    block_rows = order_rows // BLOCKS
    block_stack = jnp.transpose(sample.reshape(probe_total, BLOCKS, block_rows), (1, 0, 2))

    def compress(slab_block):
        slab_block = slab_block.astype(jnp.float32)
        gram = jnp.dot(slab_block, slab_block.T, precision=lax.Precision.HIGHEST)
        gram = gram + ridge_share * block_rows * jnp.eye(probe_total, dtype=jnp.float32)
        lower_factor = jnp.linalg.cholesky(gram)
        return lax.linalg.triangular_solve(lower_factor, slab_block, left_side=True, lower=True)
    basis_rows = lax.map(compress, block_stack)
    return jnp.transpose(basis_rows, (1, 0, 2)).reshape(probe_total, order_rows)
```

```python
import jax
import jax.numpy as jnp
from jax import lax
from jax.experimental import pallas as pl
from jax.experimental.pallas import tpu as pltpu
from jax.sharding import PartitionSpec as P

BLOCKS = 64


ridge_share = 0.05


PANEL = 16


def split2(x):
    hi = x.astype(jnp.bfloat16)
    return hi, (x - hi.astype(jnp.float32)).astype(jnp.bfloat16)


def split3(x):
    hi = x.astype(jnp.bfloat16)
    rest = x - hi.astype(jnp.float32)
    mid = rest.astype(jnp.bfloat16)
    return hi, mid, (rest - mid.astype(jnp.float32)).astype(jnp.bfloat16)


def dot32(a, b):
    return jnp.dot(a, b, preferred_element_type=jnp.float32)


def invert_factor(t_ref):
    size = t_ref.shape[0]
    m = PANEL
    sub = lax.broadcasted_iota(jnp.int32, (m, 128), 0)
    lane = lax.broadcasted_iota(jnp.int32, (m, 128), 1)
    halves = size // 128
    for p in range(size // m):
        j0 = p * m
        g, jl = j0 // 128, j0 % 128
        rows = pl.ds(j0, m)
        panel = [t_ref[rows, pl.ds(128 * h, 128)] for h in range(halves)]
        diagonal = panel[g]
        cols = [jnp.broadcast_to(diagonal[:, jl + j : jl + j + 1], (m, 128)) for j in range(m)]
        inside = (lane >= jl) & (lane < jl + m)
        panel[g] = jnp.where(inside, jnp.where(lane - jl == sub, 1.0, 0.0), diagonal)
        outs = [[] for _ in range(halves)]
        for k in range(m):
            pivot = jnp.broadcast_to(cols[k][k : k + 1, :], (m, 128))
            inverse = 1.0 / pivot
            root = lax.rsqrt(pivot[:1])
            here = sub == k
            factor = jnp.where(here, -inverse, cols[k] * inverse)
            for h in range(halves):
                row = panel[h][k : k + 1, :]
                outs[h].append(row * root)
                panel[h] = jnp.where(here, 0.0, panel[h]) - factor * row
            for j in range(k + 1, m):
                row = cols[j][k : k + 1, :]
                cols[j] = jnp.where(here, 0.0, cols[j]) - factor * row
        for h in range(halves):
            t_ref[rows, pl.ds(128 * h, 128)] = jnp.concatenate(outs[h], 0)
        left = size - j0 - m
        if left:
            rest = pl.ds(j0 + m, left)
            lh, lm, ll = split3(t_ref[rest, pl.ds(128 * g, 128)][:, jl : jl + m])
            zh, zm, zl = split3(jnp.concatenate(panel, 1))
            update = dot32(
                jnp.concatenate([lh, lm, ll, lh, lm, lh], 1),
                jnp.concatenate([zh, zh, zh, zm, zm, zl], 0),
            )
            at = lax.broadcasted_iota(jnp.int32, (left, size), 1)
            t_ref[rest, :] = jnp.where((at >= j0) & (at < j0 + m), 0.0, t_ref[rest, :]) - update


def orthonormalize(gram_ref, sample_ref, basis_ref, work_ref):
    work_ref[...] = gram_ref[...]
    invert_factor(work_ref)
    size = work_ref.shape[0]
    row_at = lax.broadcasted_iota(jnp.int32, (size, size), 0)
    col_at = lax.broadcasted_iota(jnp.int32, (size, size), 1)
    hi, lo = split2(jnp.where(col_at <= row_at, work_ref[...], 0.0))
    sample = sample_ref[...]
    basis_ref[...] = dot32(hi, sample) + dot32(lo, sample)


def from_partner(value, axis, apart):
    mask = 2**apart
    pairs = [(source, source ^ mask) for source in range(lax.axis_size(axis))]
    return lax.ppermute(value, axis, pairs)


def shards(responses, probes, left_factors, right_factors, level_ranks):
    rows_count = lax.axis_size("rows")
    local_probes, rows_dev = responses.shape
    levels_count, rank_width, _ = left_factors.shape
    rank_iota = jnp.arange(rank_width)
    partials = []
    layouts = []
    for level_index in range(levels_count):
        clusters = 2 ** (level_index + 1)
        per_device = max(1, clusters // rows_count)
        cluster_span = max(1, rows_count // clusters)
        layouts.append((clusters, per_device, cluster_span))
        right_part = right_factors[level_index].reshape(
            rank_width, per_device, rows_dev // per_device
        )
        probe_part = probes.reshape(local_probes, per_device, rows_dev // per_device)
        partials.append(
            jnp.einsum("kcn,rcn->ckr", right_part, probe_part, preferred_element_type=jnp.float32)
        )
    siblings = []
    running = list(partials)
    finished = [None] * levels_count
    span_list = []
    for level_index in range(levels_count):
        clusters, per_device, cluster_span = layouts[level_index]
        span_list.append(cluster_span.bit_length() - 1)
        if clusters > rows_count:
            swapped = partials[level_index].reshape(per_device // 2, 2, rank_width, local_probes)[
                :, ::-1
            ]
            finished[level_index] = swapped.reshape(per_device, rank_width, local_probes)
    for bit_number in range(rows_count.bit_length() - 1):
        crossing = [
            level_index
            for level_index in range(levels_count)
            if finished[level_index] is None and span_list[level_index] >= bit_number
        ]
        payload = jnp.concatenate([running[level_index] for level_index in crossing], 0)
        received = from_partner(payload, "rows", bit_number)
        for slot_number, level_index in enumerate(crossing):
            incoming = received[slot_number : slot_number + 1]
            if span_list[level_index] > bit_number:
                running[level_index] = running[level_index] + incoming
            else:
                finished[level_index] = incoming
    siblings = finished
    residual = responses.astype(jnp.float32)
    for level_index in range(levels_count):
        clusters, per_device, cluster_span = layouts[level_index]
        keep_rows = rank_iota[None, :, None] < level_ranks[level_index]
        sibling = jnp.where(keep_rows, siblings[level_index], 0.0).astype(jnp.bfloat16)
        left_part = left_factors[level_index].reshape(
            rank_width, per_device, rows_dev // per_device
        )
        update = jnp.einsum("ckr,kcn->rcn", sibling, left_part, preferred_element_type=jnp.float32)
        residual = residual - update.reshape(local_probes, rows_dev)
    sample = residual.astype(jnp.bfloat16)
    slab = lax.all_to_all(sample, "probe", split_axis=1, concat_axis=0, tiled=True)
    all_probes, slab_rows = slab.shape
    block_rows = rows_dev * rows_count // BLOCKS
    piece_rows = min(block_rows, slab_rows)
    piece_count = slab_rows // piece_rows
    piece_view = slab.reshape(all_probes, piece_count, piece_rows)
    piece_gram = jnp.einsum(
        "rpg,spg->prs", piece_view, piece_view, preferred_element_type=jnp.float32
    )
    group_size = max(1, block_rows // slab_rows)
    full_gram = piece_gram
    bit_number = 0
    full_gram = full_gram + from_partner(full_gram, "probe", bit_number)
    shifted = full_gram + ridge_share * block_rows * jnp.eye(all_probes, dtype=jnp.float32)
    return pl.pallas_call(
        orthonormalize,
        out_shape=jax.ShapeDtypeStruct(slab.shape, jnp.float32),
        in_specs=[pl.BlockSpec(memory_space=pltpu.VMEM)] * 2,
        out_specs=pl.BlockSpec(memory_space=pltpu.VMEM),
        scratch_shapes=[pltpu.VMEM((all_probes, all_probes), jnp.float32)],
        name="orthonormalize",
    )(shifted[0], slab)


def solution(mesh):
    return jax.shard_map(
        shards,
        mesh=mesh,
        in_specs=(
            P("probe", "rows"),
            P("probe", "rows"),
            P(None, None, "rows"),
            P(None, None, "rows"),
            P(),
        ),
        out_specs=P(None, ("rows", "probe")),
        check_vma=False,
    )
```

```python
import jax
import jax.numpy as jnp
from jax import lax
from jax.experimental import pallas as pl
from jax.experimental.pallas import tpu as pltpu
from jax.sharding import PartitionSpec as P

BLOCKS = 64


ridge_share = 0.05


PANEL = 16


def split2(x):
    hi = x.astype(jnp.bfloat16)
    return hi, (x - hi.astype(jnp.float32)).astype(jnp.bfloat16)


def split3(x):
    hi = x.astype(jnp.bfloat16)
    rest = x - hi.astype(jnp.float32)
    mid = rest.astype(jnp.bfloat16)
    return hi, mid, (rest - mid.astype(jnp.float32)).astype(jnp.bfloat16)


def dot32(a, b):
    return jnp.dot(a, b, preferred_element_type=jnp.float32)


def invert_factor(t_ref):
    size = t_ref.shape[0]
    m = PANEL
    sub = lax.broadcasted_iota(jnp.int32, (m, 128), 0)
    lane = lax.broadcasted_iota(jnp.int32, (m, 128), 1)
    halves = size // 128
    for p in range(size // m):
        j0 = p * m
        g, jl = j0 // 128, j0 % 128
        rows = pl.ds(j0, m)
        panel = [t_ref[rows, pl.ds(128 * h, 128)] for h in range(halves)]
        diagonal = panel[g]
        cols = [jnp.broadcast_to(diagonal[:, jl + j : jl + j + 1], (m, 128)) for j in range(m)]
        inside = (lane >= jl) & (lane < jl + m)
        panel[g] = jnp.where(inside, jnp.where(lane - jl == sub, 1.0, 0.0), diagonal)
        outs = [[] for _ in range(halves)]
        for k in range(m):
            pivot = jnp.broadcast_to(cols[k][k : k + 1, :], (m, 128))
            inverse = 1.0 / pivot
            root = lax.rsqrt(pivot[:1])
            here = sub == k
            factor = jnp.where(here, -inverse, cols[k] * inverse)
            for h in range(halves):
                row = panel[h][k : k + 1, :]
                outs[h].append(row * root)
                panel[h] = jnp.where(here, 0.0, panel[h]) - factor * row
            for j in range(k + 1, m):
                row = cols[j][k : k + 1, :]
                cols[j] = jnp.where(here, 0.0, cols[j]) - factor * row
        for h in range(halves):
            t_ref[rows, pl.ds(128 * h, 128)] = jnp.concatenate(outs[h], 0)
        left = size - j0 - m
        if left:
            rest = pl.ds(j0 + m, left)
            lh, lm, ll = split3(t_ref[rest, pl.ds(128 * g, 128)][:, jl : jl + m])
            zh, zm, zl = split3(jnp.concatenate(panel, 1))
            update = dot32(
                jnp.concatenate([lh, lm, ll, lh, lm, lh], 1),
                jnp.concatenate([zh, zh, zh, zm, zm, zl], 0),
            )
            at = lax.broadcasted_iota(jnp.int32, (left, size), 1)
            t_ref[rest, :] = jnp.where((at >= j0) & (at < j0 + m), 0.0, t_ref[rest, :]) - update


def orthonormalize(gram_ref, sample_ref, basis_ref, work_ref):
    work_ref[...] = gram_ref[...]
    invert_factor(work_ref)
    size = work_ref.shape[0]
    row_at = lax.broadcasted_iota(jnp.int32, (size, size), 0)
    col_at = lax.broadcasted_iota(jnp.int32, (size, size), 1)
    hi, lo = split2(jnp.where(col_at <= row_at, work_ref[...], 0.0))
    sample = sample_ref[...]
    basis_ref[...] = dot32(hi, sample) + dot32(lo, sample)


MESH = pl.DeviceIdType.MESH
ROWS_AXIS = 16
PROBE_AXIS = 8


def sample_kernel(
    ranks_ref,
    resp_hbm,
    probes_hbm,
    left_hbm,
    right_hbm,
    sample_out,
    gram_out,
    probes_v,
    right_v,
    left_v,
    resp_v,
    sample_v,
    sib_v,
    part_v,
    sum_v,
    near_v,
    far_v,
    last_v,
    local_sem,
    right_sem,
    near_send,
    near_recv,
    far_send,
    far_recv,
    sib_send,
    sib_recv,
    resp_send,
    resp_recv,
):
    r = lax.axis_index("rows")
    p = lax.axis_index("probe")
    core = r % 2
    high = (r // 2) % 2
    x = r // 4
    levels = right_v.shape[0]
    width = right_v.shape[1]
    local = probes_v.shape[0]
    pair_rows = resp_v.shape[1]
    half_rows = pair_rows // 2

    near = []
    for offset in (1, 2, 3):
        other = x * 4 + ((high + offset // 2) % 2) * 2 + (core + offset % 2) % 2
        near.append((other, p))
    in_plane = high * 2 + core
    x_pair = x + 1 - 2 * (x % 2)
    x_far = 2 - 2 * (x // 2)
    far = [(x_pair * 4 + in_plane, p), (x_far * 4 + in_plane, p), ((x_far + 1) * 4 + in_plane, p)]
    group = [(r, (p + d) % PROBE_AXIS) for d in range(1, PROBE_AXIS)]

    barrier = pltpu.get_barrier_semaphore()
    for peer in near + far + group:
        pl.semaphore_signal(barrier, inc=1, device_id=peer, device_id_type=MESH)

    probes_copy = pltpu.make_async_copy(probes_hbm, probes_v, local_sem.at[0])
    probes_copy.start()
    rights = [
        pltpu.make_async_copy(right_hbm.at[l], right_v.at[l], right_sem.at[l]) for l in range(levels)
    ]
    depth = 2
    for l in range(depth):
        rights[l].start()
    pair_at = pl.multiple_of((p // 2) * pair_rows, pair_rows)
    own_rows = pl.ds(pl.multiple_of(p * local, local), local)
    own_resp = pltpu.make_async_copy(
        resp_hbm.at[:, pl.ds(pair_at, pair_rows)], resp_v.at[own_rows, :], local_sem.at[1]
    )
    left_copy = pltpu.make_async_copy(
        left_hbm.at[:, :, pl.ds(pair_at, pair_rows)], left_v, local_sem.at[2]
    )

    lane = lax.broadcasted_iota(jnp.int32, (local, width), 1)

    def coupling(l, start, size):
        value = lax.dot_general(
            probes_v[:, start : start + size],
            right_v[l, :, start : start + size],
            (((1,), (1,)), ((), ())),
            preferred_element_type=jnp.float32,
        )
        return jnp.where(lane < ranks_ref[l], value, 0.0)

    def send(source, target, send_sem, recv_sem, peer):
        copy = pltpu.make_async_remote_copy(
            src_ref=source,
            dst_ref=target,
            send_sem=send_sem,
            recv_sem=recv_sem,
            device_id=peer,
            device_id_type=MESH,
        )
        copy.start()
        return copy

    def ready(l):
        rights[l].wait()
        if l + depth < levels:
            rights[l + depth].start()
        elif l + depth == levels:
            own_resp.start()
            left_copy.start()

    total = probes_v.shape[1]
    started = []
    probes_copy.wait()
    ready(0)
    part_v[0] = coupling(0, 0, total)
    pl.semaphore_wait(barrier, len(near) + len(far) + len(group))

    near_copies = [[None] * 3 for _ in range(4)]
    for i in range(3):
        near_copies[0][i] = send(
            part_v.at[0], near_v.at[0, i], near_send.at[0, i], near_recv.at[0, i], near[i]
        )
    ready(1)
    part_v[1] = coupling(1, 0, total)
    for i in range(3):
        near_copies[1][i] = send(
            part_v.at[1], near_v.at[1, i], near_send.at[1, i], near_recv.at[1, i], near[i]
        )
    ready(2)
    part_v[2] = coupling(2, 0, total)
    for i in (1, 2):
        near_copies[2][i] = send(
            part_v.at[2], near_v.at[2, i], near_send.at[2, i], near_recv.at[2, i], near[i]
        )
    resp_copies = []
    for d, peer in enumerate(group):
        at = pl.multiple_of((peer[1] // 2) * pair_rows, pair_rows)
        resp_copies.append(
            send(
                resp_hbm.at[:, pl.ds(at, pair_rows)],
                resp_v.at[own_rows, :],
                resp_send.at[d],
                resp_recv.at[d],
                peer,
            )
        )

    def block(l):
        return pl.ds(l * width, width)

    def gather(l):
        return [
            send(
                sib_v.at[own_rows, block(l)],
                sib_v.at[own_rows, block(l)],
                sib_send.at[l, d],
                sib_recv.at[l, d],
                peer,
            )
            for d, peer in enumerate(group)
        ]

    for i in range(3):
        near_copies[0][i].wait_recv()
    sum_v[0] = (part_v[0] + near_v[0, 0]) + (near_v[0, 1] + near_v[0, 2])
    far_copies = [
        send(sum_v.at[0], far_v.at[x % 2], far_send.at[i], far_recv.at[x % 2], far[1 + i])
        for i in range(2)
    ]
    ready(3)
    last_v[2] = coupling(3, 0, total).astype(jnp.bfloat16)
    near_copies[3][0] = send(
        last_v.at[2], last_v.at[3], near_send.at[3, 0], near_recv.at[3, 0], near[0]
    )
    for i in range(3):
        near_copies[1][i].wait_recv()
    sum_v[1] = (part_v[1] + near_v[1, 0]) + (near_v[1, 1] + near_v[1, 2])
    pair_copy = send(sum_v.at[1], far_v.at[2], far_send.at[2], far_recv.at[2], far[0])
    ready(4)
    for c in range(2):
        last_v[c] = coupling(4, c * (total // 2), total // 2).astype(jnp.bfloat16)
    gathers = []
    sib_v[own_rows, block(4)] = last_v[1 - p // 4]
    gathers += [
        send(
            last_v.at[1 - peer[1] // 4],
            sib_v.at[own_rows, block(4)],
            sib_send.at[4, d],
            sib_recv.at[4, d],
            peer,
        )
        for d, peer in enumerate(group)
    ]
    for i in (1, 2):
        near_copies[2][i].wait_recv()
    sib_v[own_rows, block(2)] = (near_v[2, 1] + near_v[2, 2]).astype(jnp.bfloat16)
    gathers += gather(2)
    near_copies[3][0].wait_recv()
    sib_v[own_rows, block(3)] = last_v[3]
    gathers += gather(3)
    pair_copy.wait_recv()
    sib_v[own_rows, block(1)] = far_v[2].astype(jnp.bfloat16)
    gathers += gather(1)
    for i in range(2):
        pltpu.make_async_remote_copy(
            src_ref=sum_v.at[0],
            dst_ref=far_v.at[i],
            send_sem=far_send.at[i],
            recv_sem=far_recv.at[i],
            device_id=far[1],
            device_id_type=MESH,
        ).wait_recv()
    sib_v[own_rows, block(0)] = (far_v[0] + far_v[1]).astype(jnp.bfloat16)
    gathers += gather(0)

    own_resp.wait()
    left_copy.wait()
    for copy in resp_copies:
        copy.wait_recv()
    for copy in gathers:
        copy.wait_recv()

    chunk = 512
    for c in range(pair_rows // chunk):
        at = slice(c * chunk, (c + 1) * chunk)
        update = dot32(sib_v[...], left_v[:, :, at].reshape(levels * width, chunk))
        sample_v[:, at] = (resp_v[:, at].astype(jnp.float32) - update).astype(jnp.bfloat16)
    gram = lax.dot_general(
        sample_v[...],
        sample_v[...],
        (((1,), (1,)), ((), ())),
        preferred_element_type=jnp.float32,
    )
    size = gram.shape[0]
    row_at = lax.broadcasted_iota(jnp.int32, (size, size), 0)
    col_at = lax.broadcasted_iota(jnp.int32, (size, size), 1)
    gram_out[...] = gram + jnp.where(row_at == col_at, ridge_share * pair_rows, 0.0)
    half_at = pl.multiple_of((p % 2) * half_rows, half_rows)
    sample_out[...] = sample_v[:, pl.ds(half_at, half_rows)]

    for copies in near_copies:
        for copy in copies:
            if copy is not None:
                copy.wait_send()
    for copy in far_copies + [pair_copy] + resp_copies + gathers:
        copy.wait_send()


def shards(responses, probes, left_factors, right_factors, level_ranks):
    levels, width, rows_dev = right_factors.shape
    local = probes.shape[0]
    probe_count = local * PROBE_AXIS
    block_rows = rows_dev * ROWS_AXIS // BLOCKS
    slab_rows = rows_dev // PROBE_AXIS
    vmem = pl.BlockSpec(memory_space=pltpu.VMEM)
    anywhere = pl.BlockSpec(memory_space=pl.ANY)
    bf16, f32 = jnp.bfloat16, jnp.float32
    dma = pltpu.SemaphoreType.DMA
    sample, gram = pl.pallas_call(
        sample_kernel,
        out_shape=(
            jax.ShapeDtypeStruct((probe_count, slab_rows), bf16),
            jax.ShapeDtypeStruct((probe_count, probe_count), f32),
        ),
        in_specs=[pl.BlockSpec(memory_space=pltpu.SMEM)] + [anywhere] * 4,
        out_specs=(vmem, vmem),
        scratch_shapes=[
            pltpu.VMEM((local, rows_dev), bf16),
            pltpu.VMEM((levels, width, rows_dev), bf16),
            pltpu.VMEM((levels, width, block_rows), bf16),
            pltpu.VMEM((probe_count, block_rows), bf16),
            pltpu.VMEM((probe_count, block_rows), bf16),
            pltpu.VMEM((probe_count, levels * width), bf16),
            pltpu.VMEM((3, local, width), f32),
            pltpu.VMEM((2, local, width), f32),
            pltpu.VMEM((3, 3, local, width), f32),
            pltpu.VMEM((3, local, width), f32),
            pltpu.VMEM((4, local, width), bf16),
            dma((3,)),
            dma((levels,)),
            dma((4, 3)),
            dma((4, 3)),
            dma((3,)),
            dma((3,)),
            dma((levels, PROBE_AXIS - 1)),
            dma((levels, PROBE_AXIS - 1)),
            dma((PROBE_AXIS - 1,)),
            dma((PROBE_AXIS - 1,)),
        ],
        compiler_params=pltpu.CompilerParams(collective_id=0, has_side_effects=True),
        name="sample_and_gram",
    )(level_ranks, responses, probes, left_factors, right_factors)
    return pl.pallas_call(
        orthonormalize,
        out_shape=jax.ShapeDtypeStruct(sample.shape, f32),
        in_specs=[vmem] * 2,
        out_specs=vmem,
        scratch_shapes=[pltpu.VMEM((probe_count, probe_count), f32)],
        name="orthonormalize",
    )(gram, sample)


def solution(mesh):
    return jax.shard_map(
        shards,
        mesh=mesh,
        in_specs=(
            P("probe", "rows"),
            P("probe", "rows"),
            P(None, None, "rows"),
            P(None, None, "rows"),
            P(),
        ),
        out_specs=P(None, ("rows", "probe")),
        check_vma=False,
    )
```

```python
import jax
import jax.numpy as jnp
from jax import lax
from jax.experimental import pallas as pl
from jax.experimental.pallas import tpu as pltpu
from jax.sharding import PartitionSpec as P

BLOCKS = 64


ridge_share = 0.05


PANEL = 16


def split2(x):
    hi = x.astype(jnp.bfloat16)
    return hi, (x - hi.astype(jnp.float32)).astype(jnp.bfloat16)


def split3(x):
    hi = x.astype(jnp.bfloat16)
    rest = x - hi.astype(jnp.float32)
    mid = rest.astype(jnp.bfloat16)
    return hi, mid, (rest - mid.astype(jnp.float32)).astype(jnp.bfloat16)


def dot32(a, b):
    return jnp.dot(a, b, preferred_element_type=jnp.float32)


def invert_factor(t_ref):
    size = t_ref.shape[0]
    m = PANEL
    sub = lax.broadcasted_iota(jnp.int32, (m, 128), 0)
    lane = lax.broadcasted_iota(jnp.int32, (m, 128), 1)
    halves = size // 128
    for p in range(size // m):
        j0 = p * m
        g, jl = j0 // 128, j0 % 128
        rows = pl.ds(j0, m)
        panel = [t_ref[rows, pl.ds(128 * h, 128)] for h in range(halves)]
        diagonal = panel[g]
        cols = [jnp.broadcast_to(diagonal[:, jl + j : jl + j + 1], (m, 128)) for j in range(m)]
        inside = (lane >= jl) & (lane < jl + m)
        panel[g] = jnp.where(inside, jnp.where(lane - jl == sub, 1.0, 0.0), diagonal)
        outs = [[] for _ in range(halves)]
        for k in range(m):
            pivot = jnp.broadcast_to(cols[k][k : k + 1, :], (m, 128))
            inverse = 1.0 / pivot
            root = lax.rsqrt(pivot[:1])
            here = sub == k
            factor = jnp.where(here, -inverse, cols[k] * inverse)
            for h in range(halves):
                row = panel[h][k : k + 1, :]
                outs[h].append(row * root)
                panel[h] = jnp.where(here, 0.0, panel[h]) - factor * row
            for j in range(k + 1, m):
                row = cols[j][k : k + 1, :]
                cols[j] = jnp.where(here, 0.0, cols[j]) - factor * row
        for h in range(halves):
            t_ref[rows, pl.ds(128 * h, 128)] = jnp.concatenate(outs[h], 0)
        left = size - j0 - m
        if left:
            rest = pl.ds(j0 + m, left)
            lh, lm, ll = split3(t_ref[rest, pl.ds(128 * g, 128)][:, jl : jl + m])
            zh, zm, zl = split3(jnp.concatenate(panel, 1))
            update = dot32(
                jnp.concatenate([lh, lm, ll, lh, lm, lh], 1),
                jnp.concatenate([zh, zh, zh, zm, zm, zl], 0),
            )
            at = lax.broadcasted_iota(jnp.int32, (left, size), 1)
            t_ref[rest, :] = jnp.where((at >= j0) & (at < j0 + m), 0.0, t_ref[rest, :]) - update


def orthonormalize(gram_ref, sample_ref, basis_ref, work_ref):
    work_ref[...] = gram_ref[...]
    invert_factor(work_ref)
    size = work_ref.shape[0]
    row_at = lax.broadcasted_iota(jnp.int32, (size, size), 0)
    col_at = lax.broadcasted_iota(jnp.int32, (size, size), 1)
    hi, lo = split2(jnp.where(col_at <= row_at, work_ref[...], 0.0))
    sample = sample_ref[...]
    basis_ref[...] = dot32(hi, sample) + dot32(lo, sample)


MESH = pl.DeviceIdType.MESH
ROWS_AXIS = 16
PROBE_AXIS = 8
RING = 4


def sample_kernel(
    ranks_ref,
    resp_hbm,
    probes_hbm,
    left_hbm,
    right_hbm,
    sample_out,
    gram_out,
    probes_v,
    right_v,
    left_v,
    resp_v,
    sample_v,
    sib_v,
    part_v,
    sum_v,
    near_v,
    near2_v,
    far_v,
    stage_v,
    last_v,
    local_sem,
    right_sem,
    near_send,
    near_recv,
    far_send,
    far_recv,
    sib_send,
    sib_recv,
    ring_send,
    ring_recv,
    forward_send,
    forward_recv,
    cross_send,
    cross_recv,
):
    r = lax.axis_index("rows")
    p = lax.axis_index("probe")
    core = r % 2
    high = (r // 2) % 2
    x = r // 4
    z = p // RING
    y = p % RING
    levels = right_v.shape[0]
    width = right_v.shape[1]
    local = probes_v.shape[0]
    pair_rows = resp_v.shape[2]
    half_rows = pair_rows // 2

    near = []
    for offset in (1, 2, 3):
        other = x * 4 + ((high + offset // 2) % 2) * 2 + (core + offset % 2) % 2
        near.append((other, p))
    in_plane = high * 2 + core
    x_pair = x + 1 - 2 * (x % 2)
    x_far = 2 - 2 * (x // 2)
    far = [(x_pair * 4 + in_plane, p), (x_far * 4 + in_plane, p), ((x_far + 1) * 4 + in_plane, p)]
    group = [(r, (p + d) % PROBE_AXIS) for d in range(1, PROBE_AXIS)]
    ring = [(r, z * RING + (y + d) % RING) for d in range(1, RING)]
    across = (r, (1 - z) * RING + y)

    barrier = pltpu.get_barrier_semaphore()
    for peer in near + far + group:
        pl.semaphore_signal(barrier, inc=1, device_id=peer, device_id_type=MESH)

    probes_copy = pltpu.make_async_copy(probes_hbm, probes_v, local_sem.at[0])
    probes_copy.start()
    rights = [
        pltpu.make_async_copy(right_hbm.at[l], right_v.at[l], right_sem.at[l]) for l in range(levels)
    ]
    depth = 2
    rights[0].start()

    def pair_columns(pair):
        return pl.ds(pl.multiple_of(pair * pair_rows, pair_rows), pair_rows)

    own_pair = y // 2
    own_rows = pl.ds(pl.multiple_of(p * local, local), local)
    across_rows = pl.ds(pl.multiple_of(across[1] * local, local), local)
    own_columns = pair_columns(p // 2)
    own_resp = pltpu.make_async_copy(
        resp_hbm.at[:, own_columns], resp_v.at[own_pair, own_rows, :], local_sem.at[1]
    )
    left_copy = pltpu.make_async_copy(left_hbm.at[:, :, own_columns], left_v, local_sem.at[2])

    lane = lax.broadcasted_iota(jnp.int32, (local, width), 1)

    def coupling(l, start, size):
        value = lax.dot_general(
            probes_v[:, start : start + size],
            right_v[l, :, start : start + size],
            (((1,), (1,)), ((), ())),
            preferred_element_type=jnp.float32,
        )
        return jnp.where(lane < ranks_ref[l], value, 0.0)

    def send(source, target, send_sem, recv_sem, peer):
        copy = pltpu.make_async_remote_copy(
            src_ref=source,
            dst_ref=target,
            send_sem=send_sem,
            recv_sem=recv_sem,
            device_id=peer,
            device_id_type=MESH,
        )
        copy.start()
        return copy

    def ready(l):
        rights[l].wait()
        if l == 0:
            rights[1].start()
        if l + depth < levels:
            rights[l + depth].start()
        elif l + depth == levels:
            own_resp.start()
            left_copy.start()

    def cross(i):
        half = i % 2
        pair = (own_pair + 1 + i // 2) % 2
        columns = pl.ds(
            pl.multiple_of(((1 - z) * 2 + pair) * pair_rows + half * half_rows, half_rows), half_rows
        )
        return send(
            resp_hbm.at[:, columns],
            resp_v.at[pair, own_rows, pl.ds(half * half_rows, half_rows)],
            cross_send.at[i],
            cross_recv.at[i],
            across,
        )

    total = probes_v.shape[1]
    probes_copy.wait()
    ready(0)
    part_v[0] = coupling(0, 0, total)
    pl.semaphore_wait(barrier, len(near) + len(far) + len(group))

    near_copies = [
        send(part_v.at[0], near_v.at[i], near_send.at[0, i], near_recv.at[0, i], near[i])
        for i in range(3)
    ]
    crossing = [cross(0)]
    ring_copies = []
    for d, peer in enumerate(ring):
        pair = (peer[1] % RING) // 2
        ring_copies.append(
            send(
                resp_hbm.at[:, pair_columns(peer[1] // 2)],
                resp_v.at[pair, own_rows, :],
                ring_send.at[0, d],
                ring_recv.at[0, d],
                peer,
            )
        )
    ready(1)
    part_v[1] = coupling(1, 0, total)
    crossing.append(cross(1))
    ready(2)
    part_v[2] = coupling(2, 0, total)
    near2_copies = [
        send(
            part_v.at[pl.ds(1, 2)], near2_v.at[i], near_send.at[1, i], near_recv.at[1, i], near[i]
        )
        for i in range(3)
    ]
    crossing += [cross(2), cross(3)]
    ready(3)
    last_v[0] = coupling(3, 0, total).astype(jnp.bfloat16)
    core_copy = send(last_v.at[0], last_v.at[1], near_send.at[2, 0], near_recv.at[2, 0], near[0])
    ready(4)
    for c in range(2):
        stage_v[1 - c, :, 2 * width : 3 * width] = coupling(
            4, c * (total // 2), total // 2
        ).astype(jnp.bfloat16)

    forwards = []

    def forward_other(half):
        crossing[half].wait_recv()
        place = pl.ds(half * half_rows, half_rows)
        other = (own_pair + 1) % 2
        for member in range(2):
            peer = (r, z * RING + other * 2 + member)
            forwards.append(
                pltpu.make_async_remote_copy(
                    src_ref=resp_v.at[other, across_rows, place],
                    dst_ref=resp_v.at[other, across_rows, place],
                    send_sem=forward_send.at[half, member],
                    recv_sem=forward_recv.at[half, y % 2],
                    device_id=peer,
                    device_id_type=MESH,
                )
            )
            forwards[-1].start()

    def forward_own(half):
        crossing[2 + half].wait_recv()
        place = pl.ds(half * half_rows, half_rows)
        peer = (r, p + 1 - 2 * (y % 2))
        forwards.append(
            send(
                resp_v.at[own_pair, across_rows, place],
                resp_v.at[own_pair, across_rows, place],
                forward_send.at[half, 2],
                forward_recv.at[half, 2],
                peer,
            )
        )

    forward_other(0)
    forward_other(1)
    for copy in near_copies:
        copy.wait_recv()
    sum_v[0] = (part_v[0] + near_v[0]) + (near_v[1] + near_v[2])
    far_copies = [
        send(sum_v.at[0], far_v.at[x % 2], far_send.at[i], far_recv.at[x % 2], far[1 + i])
        for i in range(2)
    ]
    for copy in near2_copies:
        copy.wait_recv()
    sum_v[1] = (part_v[1] + near2_v[0, 0]) + (near2_v[1, 0] + near2_v[2, 0])
    pair_copy = send(sum_v.at[1], far_v.at[2], far_send.at[2], far_recv.at[2], far[0])
    forward_own(0)
    core_copy.wait_recv()
    level3 = (near2_v[1, 1] + near2_v[2, 1]).astype(jnp.bfloat16)
    for c in range(2):
        stage_v[c, :, :width] = level3
        stage_v[c, :, width : 2 * width] = last_v[1]

    def columns_of(first, count):
        return pl.ds(first * width, count * width)

    gathers = [
        send(
            stage_v.at[peer[1] // RING],
            sib_v.at[own_rows, columns_of(2, 3)],
            sib_send.at[0, d],
            sib_recv.at[0, d],
            peer,
        )
        for d, peer in enumerate(group)
    ]
    sib_v[own_rows, columns_of(2, 3)] = stage_v[z]

    forward_own(1)
    pair_copy.wait_recv()
    sib_v[own_rows, columns_of(1, 1)] = far_v[2].astype(jnp.bfloat16)
    for i in range(2):
        pltpu.make_async_remote_copy(
            src_ref=sum_v.at[0],
            dst_ref=far_v.at[i],
            send_sem=far_send.at[i],
            recv_sem=far_recv.at[i],
            device_id=far[1],
            device_id_type=MESH,
        ).wait_recv()
    sib_v[own_rows, columns_of(0, 1)] = (far_v[0] + far_v[1]).astype(jnp.bfloat16)
    gathers += [
        send(
            sib_v.at[own_rows, columns_of(0, 2)],
            sib_v.at[own_rows, columns_of(0, 2)],
            sib_send.at[1, d],
            sib_recv.at[1, d],
            peer,
        )
        for d, peer in enumerate(group)
    ]

    own_resp.wait()
    left_copy.wait()
    for copy in ring_copies + gathers:
        copy.wait_recv()
    for half in range(2):
        place = pl.ds(half * half_rows, half_rows)
        for member in range(3):
            pltpu.make_async_remote_copy(
                src_ref=resp_v.at[own_pair, across_rows, place],
                dst_ref=resp_v.at[own_pair, across_rows, place],
                send_sem=forward_send.at[half, member],
                recv_sem=forward_recv.at[half, member],
                device_id=across,
                device_id_type=MESH,
            ).wait_recv()

    chunk = 512
    for c in range(pair_rows // chunk):
        at = slice(c * chunk, (c + 1) * chunk)
        update = dot32(sib_v[...], left_v[:, :, at].reshape(levels * width, chunk))
        sample_v[:, at] = (resp_v[own_pair, :, at].astype(jnp.float32) - update).astype(jnp.bfloat16)
    gram = lax.dot_general(
        sample_v[...],
        sample_v[...],
        (((1,), (1,)), ((), ())),
        preferred_element_type=jnp.float32,
    )
    size = gram.shape[0]
    row_at = lax.broadcasted_iota(jnp.int32, (size, size), 0)
    col_at = lax.broadcasted_iota(jnp.int32, (size, size), 1)
    gram_out[...] = gram + jnp.where(row_at == col_at, ridge_share * pair_rows, 0.0)
    half_at = pl.multiple_of((p % 2) * half_rows, half_rows)
    sample_out[...] = sample_v[:, pl.ds(half_at, half_rows)]

    sent = near_copies + near2_copies + [core_copy] + far_copies + [pair_copy]
    for copy in sent + ring_copies + crossing + forwards + gathers:
        copy.wait_send()


def shards(responses, probes, left_factors, right_factors, level_ranks):
    levels, width, rows_dev = right_factors.shape
    local = probes.shape[0]
    probe_count = local * PROBE_AXIS
    block_rows = rows_dev * ROWS_AXIS // BLOCKS
    slab_rows = rows_dev // PROBE_AXIS
    vmem = pl.BlockSpec(memory_space=pltpu.VMEM)
    anywhere = pl.BlockSpec(memory_space=pl.ANY)
    bf16, f32 = jnp.bfloat16, jnp.float32
    dma = pltpu.SemaphoreType.DMA
    sample, gram = pl.pallas_call(
        sample_kernel,
        out_shape=(
            jax.ShapeDtypeStruct((probe_count, slab_rows), bf16),
            jax.ShapeDtypeStruct((probe_count, probe_count), f32),
        ),
        in_specs=[pl.BlockSpec(memory_space=pltpu.SMEM)] + [anywhere] * 4,
        out_specs=(vmem, vmem),
        scratch_shapes=[
            pltpu.VMEM((local, rows_dev), bf16),
            pltpu.VMEM((levels, width, rows_dev), bf16),
            pltpu.VMEM((levels, width, block_rows), bf16),
            pltpu.VMEM((2, probe_count, block_rows), bf16),
            pltpu.VMEM((probe_count, block_rows), bf16),
            pltpu.VMEM((probe_count, levels * width), bf16),
            pltpu.VMEM((3, local, width), f32),
            pltpu.VMEM((2, local, width), f32),
            pltpu.VMEM((3, local, width), f32),
            pltpu.VMEM((3, 2, local, width), f32),
            pltpu.VMEM((3, local, width), f32),
            pltpu.VMEM((2, local, 3 * width), bf16),
            pltpu.VMEM((2, local, width), bf16),
            dma((3,)),
            dma((levels,)),
            dma((3, 3)),
            dma((3, 3)),
            dma((3,)),
            dma((3,)),
            dma((2, PROBE_AXIS - 1)),
            dma((2, PROBE_AXIS - 1)),
            dma((1, RING - 1)),
            dma((1, RING - 1)),
            dma((2, 3)),
            dma((2, 3)),
            dma((4,)),
            dma((4,)),
        ],
        compiler_params=pltpu.CompilerParams(collective_id=0, has_side_effects=True),
        name="sample_and_gram",
    )(level_ranks, responses, probes, left_factors, right_factors)
    return pl.pallas_call(
        orthonormalize,
        out_shape=jax.ShapeDtypeStruct(sample.shape, f32),
        in_specs=[vmem] * 2,
        out_specs=vmem,
        scratch_shapes=[pltpu.VMEM((probe_count, probe_count), f32)],
        name="orthonormalize",
    )(gram, sample)


def solution(mesh):
    return jax.shard_map(
        shards,
        mesh=mesh,
        in_specs=(
            P("probe", "rows"),
            P("probe", "rows"),
            P(None, None, "rows"),
            P(None, None, "rows"),
            P(),
        ),
        out_specs=P(None, ("rows", "probe")),
        check_vma=False,
    )
```

```python
import jax
import jax.numpy as jnp
from jax import lax
from jax.experimental import pallas as pl
from jax.experimental.pallas import tpu as pltpu
from jax.sharding import PartitionSpec as P

BLOCKS = 64


ridge_share = 0.05


PANEL = 16


def split2(x):
    hi = x.astype(jnp.bfloat16)
    return hi, (x - hi.astype(jnp.float32)).astype(jnp.bfloat16)


def split3(x):
    hi = x.astype(jnp.bfloat16)
    rest = x - hi.astype(jnp.float32)
    mid = rest.astype(jnp.bfloat16)
    return hi, mid, (rest - mid.astype(jnp.float32)).astype(jnp.bfloat16)


def dot32(a, b):
    return jnp.dot(a, b, preferred_element_type=jnp.float32)


def invert_factor(t_ref):
    size = t_ref.shape[0]
    m = PANEL
    sub = lax.broadcasted_iota(jnp.int32, (8, 128), 0)
    lane = lax.broadcasted_iota(jnp.int32, (8, 128), 1)
    halves = range(size // 128)
    groups = range(m // 8)

    def spread(value, k):
        return jnp.broadcast_to(value[k : k + 1, :], (8, 128))

    for p in range(size // m):
        j0 = p * m
        g, jl = j0 // 128, j0 % 128
        panel = [
            [t_ref[pl.ds(j0 + 8 * q, 8), pl.ds(128 * h, 128)] for q in groups] for h in halves
        ]
        cols = [
            [jnp.broadcast_to(panel[g][q][:, jl + j : jl + j + 1], (8, 128)) for q in groups]
            for j in range(m)
        ]
        inside = (lane >= jl) & (lane < jl + m)
        for q in groups:
            identity = jnp.where(lane - jl - 8 * q == sub, 1.0, 0.0)
            panel[g][q] = jnp.where(inside, identity, panel[g][q])
        outs = [[] for _ in halves]
        for k in range(m):
            at, row = k // 8, k % 8
            pivot = spread(cols[k][at], row)
            inverse = 1.0 / pivot
            root = lax.rsqrt(pivot)
            here = sub == row
            factor = [cols[k][q] * inverse for q in groups]
            factor[at] = jnp.where(here, -inverse, factor[at])
            for j in range(k + 1, m):
                line = spread(cols[j][at], row)
                for q in groups:
                    base = jnp.where(here, 0.0, cols[j][q]) if q == at else cols[j][q]
                    if j == k + 1:
                        lead = jnp.where(here, -1.0, cols[k][q]) if q == at else cols[k][q]
                        cols[j][q] = base - (lead * line) * inverse
                    else:
                        cols[j][q] = base - factor[q] * line
            for h in halves:
                line = spread(panel[h][at], row)
                outs[h].append((line * root)[:1])
                for q in groups:
                    base = jnp.where(here, 0.0, panel[h][q]) if q == at else panel[h][q]
                    panel[h][q] = base - factor[q] * line
        for h in halves:
            t_ref[pl.ds(j0, m), pl.ds(128 * h, 128)] = jnp.concatenate(outs[h], 0)
        left = size - j0 - m
        if left:
            rest = pl.ds(j0 + m, left)
            lh, lm, ll = split3(t_ref[rest, pl.ds(128 * g, 128)][:, jl : jl + m])
            zh, zm, zl = split3(
                jnp.concatenate([jnp.concatenate(panel[h], 0) for h in halves], 1)
            )
            update = dot32(
                jnp.concatenate([lh, lm, ll, lh, lm, lh], 1),
                jnp.concatenate([zh, zh, zh, zm, zm, zl], 0),
            )
            at = lax.broadcasted_iota(jnp.int32, (left, size), 1)
            t_ref[rest, :] = jnp.where((at >= j0) & (at < j0 + m), 0.0, t_ref[rest, :]) - update


def orthonormalize(gram_ref, sample_ref, basis_hbm, work_ref, basis_v, sems):
    work_ref[...] = gram_ref[...]
    invert_factor(work_ref)
    size = work_ref.shape[0]
    row_at = lax.broadcasted_iota(jnp.int32, (size, size), 0)
    col_at = lax.broadcasted_iota(jnp.int32, (size, size), 1)
    hi, lo = split2(jnp.where(col_at <= row_at, work_ref[...], 0.0))
    copies = []
    for c in range(sample_ref.shape[1] // 256):
        at = pl.ds(c * 256, 256)
        sample = sample_ref[:, at]
        basis_v[:, at] = dot32(hi, sample) + dot32(lo, sample)
        copies.append(
            pltpu.make_async_copy(basis_v.at[:, at], basis_hbm.at[:, at], sems.at[c])
        )
        copies[-1].start()
    for copy in copies:
        copy.wait()


MESH = pl.DeviceIdType.MESH
ROWS_AXIS = 16
PROBE_AXIS = 8
RING = 4


def sample_kernel(
    ranks_ref,
    resp_hbm,
    probes_hbm,
    left_hbm,
    right_hbm,
    sample_out,
    gram_out,
    probes_v,
    right_v,
    left_v,
    resp_v,
    sample_v,
    sib_v,
    late_v,
    part_v,
    sum_v,
    near_v,
    near2_v,
    far_v,
    stage_v,
    last_v,
    local_sem,
    right_sem,
    near_send,
    near_recv,
    far_send,
    far_recv,
    sib_send,
    sib_recv,
    ring_send,
    ring_recv,
    forward_send,
    forward_recv,
    cross_send,
    cross_recv,
):
    r = lax.axis_index("rows")
    p = lax.axis_index("probe")
    core = r % 2
    high = (r // 2) % 2
    x = r // 4
    z = p // RING
    y = p % RING
    levels = right_v.shape[0]
    width = right_v.shape[1]
    local = probes_v.shape[0]
    pair_rows = resp_v.shape[2]
    half_rows = pair_rows // 2

    near = []
    for offset in (1, 2, 3):
        other = x * 4 + ((high + offset // 2) % 2) * 2 + (core + offset % 2) % 2
        near.append((other, p))
    in_plane = high * 2 + core
    x_pair = x + 1 - 2 * (x % 2)
    x_far = 2 - 2 * (x // 2)
    far = [(x_pair * 4 + in_plane, p), (x_far * 4 + in_plane, p), ((x_far + 1) * 4 + in_plane, p)]
    group = [(r, (p + d) % PROBE_AXIS) for d in range(1, PROBE_AXIS)]
    ring = [(r, z * RING + (y + d) % RING) for d in range(1, RING)]
    across = (r, (1 - z) * RING + y)

    barrier = pltpu.get_barrier_semaphore()
    for peer in near + far + group:
        pl.semaphore_signal(barrier, inc=1, device_id=peer, device_id_type=MESH)

    probes_copy = pltpu.make_async_copy(probes_hbm, probes_v, local_sem.at[0])
    probes_copy.start()
    rights = [
        pltpu.make_async_copy(right_hbm.at[l], right_v.at[l], right_sem.at[l]) for l in range(levels)
    ]
    depth = 2
    rights[0].start()

    def pair_columns(pair):
        return pl.ds(pl.multiple_of(pair * pair_rows, pair_rows), pair_rows)

    own_pair = y // 2
    own_rows = pl.ds(pl.multiple_of(p * local, local), local)
    across_rows = pl.ds(pl.multiple_of(across[1] * local, local), local)
    own_columns = pair_columns(p // 2)
    own_resp = pltpu.make_async_copy(
        resp_hbm.at[:, own_columns], resp_v.at[own_pair, own_rows, :], local_sem.at[1]
    )
    left_copy = pltpu.make_async_copy(left_hbm.at[:, :, own_columns], left_v, local_sem.at[2])

    lane = lax.broadcasted_iota(jnp.int32, (local, width), 1)

    def coupling(l, start, size):
        value = lax.dot_general(
            probes_v[:, start : start + size],
            right_v[l, :, start : start + size],
            (((1,), (1,)), ((), ())),
            preferred_element_type=jnp.float32,
        )
        return jnp.where(lane < ranks_ref[l], value, 0.0)

    def send(source, target, send_sem, recv_sem, peer):
        copy = pltpu.make_async_remote_copy(
            src_ref=source,
            dst_ref=target,
            send_sem=send_sem,
            recv_sem=recv_sem,
            device_id=peer,
            device_id_type=MESH,
        )
        copy.start()
        return copy

    def ready(l):
        rights[l].wait()
        if l == 0:
            rights[1].start()
        if l + depth < levels:
            rights[l + depth].start()
        elif l + depth == levels:
            own_resp.start()
            left_copy.start()

    def cross(i):
        half = i % 2
        pair = (own_pair + 1 + i // 2) % 2
        columns = pl.ds(
            pl.multiple_of(((1 - z) * 2 + pair) * pair_rows + half * half_rows, half_rows), half_rows
        )
        return send(
            resp_hbm.at[:, columns],
            resp_v.at[pair, own_rows, pl.ds(half * half_rows, half_rows)],
            cross_send.at[i],
            cross_recv.at[i],
            across,
        )

    total = probes_v.shape[1]
    probes_copy.wait()
    ready(0)
    part_v[0] = coupling(0, 0, total)
    pl.semaphore_wait(barrier, len(near) + len(far) + len(group))

    near_copies = [
        send(part_v.at[0], near_v.at[i], near_send.at[0, i], near_recv.at[0, i], near[i])
        for i in range(3)
    ]
    crossing = [cross(0)]
    ring_copies = []
    for d, peer in enumerate(ring):
        pair = (peer[1] % RING) // 2
        ring_copies.append(
            send(
                resp_hbm.at[:, pair_columns(peer[1] // 2)],
                resp_v.at[pair, own_rows, :],
                ring_send.at[0, d],
                ring_recv.at[0, d],
                peer,
            )
        )
    ready(1)
    part_v[1] = coupling(1, 0, total)
    near2_copies = [
        send(part_v.at[1], near2_v.at[i, 0], near_send.at[1, i], near_recv.at[1, i], near[i])
        for i in range(3)
    ]
    crossing.append(cross(1))
    ready(2)
    part_v[2] = coupling(2, 0, total)
    near3_copies = [
        send(part_v.at[2], near2_v.at[i, 1], near_send.at[2, i], near_recv.at[2, i], near[i])
        for i in (1, 2)
    ]
    crossing += [cross(2), cross(3)]
    ready(3)
    last_v[0] = coupling(3, 0, total).astype(jnp.bfloat16)
    core_copy = send(last_v.at[0], last_v.at[1], near_send.at[2, 0], near_recv.at[2, 0], near[0])
    ready(4)
    for c in range(2):
        stage_v[1 - c, :, 2 * width : 3 * width] = coupling(
            4, c * (total // 2), total // 2
        ).astype(jnp.bfloat16)

    forwards = []

    def forward_other(half):
        crossing[half].wait_recv()
        place = pl.ds(half * half_rows, half_rows)
        other = (own_pair + 1) % 2
        for member in range(2):
            peer = (r, z * RING + other * 2 + member)
            forwards.append(
                pltpu.make_async_remote_copy(
                    src_ref=resp_v.at[other, across_rows, place],
                    dst_ref=resp_v.at[other, across_rows, place],
                    send_sem=forward_send.at[half, member],
                    recv_sem=forward_recv.at[half, y % 2],
                    device_id=peer,
                    device_id_type=MESH,
                )
            )
            forwards[-1].start()

    def forward_own(half):
        crossing[2 + half].wait_recv()
        place = pl.ds(half * half_rows, half_rows)
        peer = (r, p + 1 - 2 * (y % 2))
        forwards.append(
            send(
                resp_v.at[own_pair, across_rows, place],
                resp_v.at[own_pair, across_rows, place],
                forward_send.at[half, 2],
                forward_recv.at[half, 2],
                peer,
            )
        )

    forward_other(0)
    for copy in near_copies:
        copy.wait_recv()
    sum_v[0] = (part_v[0] + near_v[0]) + (near_v[1] + near_v[2])
    far_copies = [
        send(sum_v.at[0], far_v.at[x % 2], far_send.at[i], far_recv.at[x % 2], far[1 + i])
        for i in range(2)
    ]
    forward_other(1)
    for copy in near2_copies:
        copy.wait_recv()
    sum_v[1] = (part_v[1] + near2_v[0, 0]) + (near2_v[1, 0] + near2_v[2, 0])
    pair_copy = send(sum_v.at[1], far_v.at[2], far_send.at[2], far_recv.at[2], far[0])
    forward_own(0)
    core_copy.wait_recv()
    for copy in near3_copies:
        copy.wait_recv()
    level3 = (near2_v[1, 1] + near2_v[2, 1]).astype(jnp.bfloat16)
    for c in range(2):
        stage_v[c, :, :width] = level3
        stage_v[c, :, width : 2 * width] = last_v[1]

    def columns_of(first, count):
        return pl.ds(first * width, count * width)

    gathers = [
        send(
            stage_v.at[peer[1] // RING],
            sib_v.at[own_rows, columns_of(2, 3)],
            sib_send.at[0, d],
            sib_recv.at[0, d],
            peer,
        )
        for d, peer in enumerate(group)
    ]
    sib_v[own_rows, columns_of(2, 3)] = stage_v[z]

    forward_own(1)
    pair_copy.wait_recv()
    sib_v[own_rows, columns_of(1, 1)] = far_v[2].astype(jnp.bfloat16)
    for i in range(2):
        pltpu.make_async_remote_copy(
            src_ref=sum_v.at[0],
            dst_ref=far_v.at[i],
            send_sem=far_send.at[i],
            recv_sem=far_recv.at[i],
            device_id=far[1],
            device_id_type=MESH,
        ).wait_recv()
    sib_v[own_rows, columns_of(0, 1)] = (far_v[0] + far_v[1]).astype(jnp.bfloat16)
    gathers += [
        send(
            sib_v.at[own_rows, columns_of(0, 2)],
            sib_v.at[own_rows, columns_of(0, 2)],
            sib_send.at[1, d],
            sib_recv.at[1, d],
            peer,
        )
        for d, peer in enumerate(group)
    ]

    own_resp.wait()
    left_copy.wait()
    for copy in gathers[: len(group)]:
        copy.wait_recv()
    chunk = 512

    def update_of(first, count, at):
        siblings = sib_v[:, first * width : (first + count) * width]
        factors = left_v[first : first + count, :, at].reshape(count * width, chunk)
        return dot32(siblings, factors)

    for c in range(pair_rows // chunk):
        at = slice(c * chunk, (c + 1) * chunk)
        late_v[:, at] = update_of(2, 3, at)
    for copy in ring_copies + gathers[len(group) :]:
        copy.wait_recv()
    for half in range(2):
        place = pl.ds(half * half_rows, half_rows)
        for member in range(3):
            pltpu.make_async_remote_copy(
                src_ref=resp_v.at[own_pair, across_rows, place],
                dst_ref=resp_v.at[own_pair, across_rows, place],
                send_sem=forward_send.at[half, member],
                recv_sem=forward_recv.at[half, member],
                device_id=across,
                device_id_type=MESH,
            ).wait_recv()

    for c in range(pair_rows // chunk):
        at = slice(c * chunk, (c + 1) * chunk)
        update = update_of(0, 2, at) + late_v[:, at]
        sample_v[:, at] = (resp_v[own_pair, :, at].astype(jnp.float32) - update).astype(jnp.bfloat16)
    gram = lax.dot_general(
        sample_v[...],
        sample_v[...],
        (((1,), (1,)), ((), ())),
        preferred_element_type=jnp.float32,
    )
    size = gram.shape[0]
    row_at = lax.broadcasted_iota(jnp.int32, (size, size), 0)
    col_at = lax.broadcasted_iota(jnp.int32, (size, size), 1)
    gram_out[...] = gram + jnp.where(row_at == col_at, ridge_share * pair_rows, 0.0)
    half_at = pl.multiple_of((p % 2) * half_rows, half_rows)
    sample_out[...] = sample_v[:, pl.ds(half_at, half_rows)]

    sent = near_copies + near2_copies + near3_copies + [core_copy] + far_copies + [pair_copy]
    for copy in sent + ring_copies + crossing + forwards + gathers:
        copy.wait_send()


def shards(responses, probes, left_factors, right_factors, level_ranks):
    levels, width, rows_dev = right_factors.shape
    local = probes.shape[0]
    probe_count = local * PROBE_AXIS
    block_rows = rows_dev * ROWS_AXIS // BLOCKS
    slab_rows = rows_dev // PROBE_AXIS
    vmem = pl.BlockSpec(memory_space=pltpu.VMEM)
    anywhere = pl.BlockSpec(memory_space=pl.ANY)
    bf16, f32 = jnp.bfloat16, jnp.float32
    dma = pltpu.SemaphoreType.DMA
    sample, gram = pl.pallas_call(
        sample_kernel,
        out_shape=(
            jax.ShapeDtypeStruct((probe_count, slab_rows), bf16),
            jax.ShapeDtypeStruct((probe_count, probe_count), f32),
        ),
        in_specs=[pl.BlockSpec(memory_space=pltpu.SMEM)] + [anywhere] * 4,
        out_specs=(vmem, vmem),
        scratch_shapes=[
            pltpu.VMEM((local, rows_dev), bf16),
            pltpu.VMEM((levels, width, rows_dev), bf16),
            pltpu.VMEM((levels, width, block_rows), bf16),
            pltpu.VMEM((2, probe_count, block_rows), bf16),
            pltpu.VMEM((probe_count, block_rows), bf16),
            pltpu.VMEM((probe_count, levels * width), bf16),
            pltpu.VMEM((probe_count, block_rows), f32),
            pltpu.VMEM((3, local, width), f32),
            pltpu.VMEM((2, local, width), f32),
            pltpu.VMEM((3, local, width), f32),
            pltpu.VMEM((3, 2, local, width), f32),
            pltpu.VMEM((3, local, width), f32),
            pltpu.VMEM((2, local, 3 * width), bf16),
            pltpu.VMEM((2, local, width), bf16),
            dma((3,)),
            dma((levels,)),
            dma((3, 3)),
            dma((3, 3)),
            dma((3,)),
            dma((3,)),
            dma((2, PROBE_AXIS - 1)),
            dma((2, PROBE_AXIS - 1)),
            dma((1, RING - 1)),
            dma((1, RING - 1)),
            dma((2, 3)),
            dma((2, 3)),
            dma((4,)),
            dma((4,)),
        ],
        compiler_params=pltpu.CompilerParams(collective_id=0, has_side_effects=True),
        name="sample_and_gram",
    )(level_ranks, responses, probes, left_factors, right_factors)
    return pl.pallas_call(
        orthonormalize,
        out_shape=jax.ShapeDtypeStruct(sample.shape, f32),
        in_specs=[vmem] * 2,
        out_specs=anywhere,
        scratch_shapes=[
            pltpu.VMEM((probe_count, probe_count), f32),
            pltpu.VMEM(sample.shape, f32),
            dma((sample.shape[1] // 256,)),
        ],
        compiler_params=pltpu.CompilerParams(

        ),
        name="orthonormalize",
    )(gram, sample)


def solution(mesh):
    return jax.shard_map(
        shards,
        mesh=mesh,
        in_specs=(
            P("probe", "rows"),
            P("probe", "rows"),
            P(None, None, "rows"),
            P(None, None, "rows"),
            P(),
        ),
        out_specs=P(None, ("rows", "probe")),
        check_vma=False,
    )
```

```python
import jax
import jax.numpy as jnp
from jax import lax
from jax.experimental import pallas as pl
from jax.experimental.pallas import tpu as pltpu
from jax.sharding import PartitionSpec as P

BLOCKS = 64


ridge_share = 0.05


PANEL = 16


def split2(x):
    hi = x.astype(jnp.bfloat16)
    return hi, (x - hi.astype(jnp.float32)).astype(jnp.bfloat16)


def split3(x):
    hi = x.astype(jnp.bfloat16)
    rest = x - hi.astype(jnp.float32)
    mid = rest.astype(jnp.bfloat16)
    return hi, mid, (rest - mid.astype(jnp.float32)).astype(jnp.bfloat16)


def dot32(a, b):
    return jnp.dot(a, b, preferred_element_type=jnp.float32)


def invert_factor(t_ref):
    size = t_ref.shape[0]
    m = PANEL
    sub = lax.broadcasted_iota(jnp.int32, (8, 128), 0)
    lane = lax.broadcasted_iota(jnp.int32, (8, 128), 1)
    halves = range(size // 128)
    groups = range(m // 8)

    def spread(value, k):
        return jnp.broadcast_to(value[k : k + 1, :], (8, 128))

    for p in range(size // m):
        j0 = p * m
        g, jl = j0 // 128, j0 % 128
        panel = [
            [t_ref[pl.ds(j0 + 8 * q, 8), pl.ds(128 * h, 128)] for q in groups] for h in halves
        ]
        cols = [
            [jnp.broadcast_to(panel[g][q][:, jl + j : jl + j + 1], (8, 128)) for q in groups]
            for j in range(m)
        ]
        inside = (lane >= jl) & (lane < jl + m)
        for q in groups:
            identity = jnp.where(lane - jl - 8 * q == sub, 1.0, 0.0)
            panel[g][q] = jnp.where(inside, identity, panel[g][q])
        outs = [[] for _ in halves]
        for k in range(m):
            at, row = k // 8, k % 8
            pivot = spread(cols[k][at], row)
            inverse = 1.0 / pivot
            root = lax.rsqrt(pivot)
            here = sub == row
            factor = [cols[k][q] * inverse for q in groups]
            factor[at] = jnp.where(here, -inverse, factor[at])
            for j in range(k + 1, m):
                line = spread(cols[j][at], row)
                for q in groups:
                    base = jnp.where(here, 0.0, cols[j][q]) if q == at else cols[j][q]
                    if j == k + 1:
                        lead = jnp.where(here, -1.0, cols[k][q]) if q == at else cols[k][q]
                        cols[j][q] = base - (lead * line) * inverse
                    else:
                        cols[j][q] = base - factor[q] * line
            for h in halves:
                line = spread(panel[h][at], row)
                outs[h].append((line * root)[:1])
                for q in groups:
                    base = jnp.where(here, 0.0, panel[h][q]) if q == at else panel[h][q]
                    panel[h][q] = base - factor[q] * line
        for h in halves:
            t_ref[pl.ds(j0, m), pl.ds(128 * h, 128)] = jnp.concatenate(outs[h], 0)
        left = size - j0 - m
        if left:
            rest = pl.ds(j0 + m, left)
            lh, lm, ll = split3(t_ref[rest, pl.ds(128 * g, 128)][:, jl : jl + m])
            zh, zm, zl = split3(
                jnp.concatenate([jnp.concatenate(panel[h], 0) for h in halves], 1)
            )
            update = dot32(
                jnp.concatenate([lh, lm, ll, lh, lm, lh], 1),
                jnp.concatenate([zh, zh, zh, zm, zm, zl], 0),
            )
            at = lax.broadcasted_iota(jnp.int32, (left, size), 1)
            t_ref[rest, :] = jnp.where((at >= j0) & (at < j0 + m), 0.0, t_ref[rest, :]) - update


def orthonormalize(gram_ref, sample_ref, basis_hbm, work_ref, basis_v, sems):
    work_ref[...] = gram_ref[...]
    invert_factor(work_ref)
    size = work_ref.shape[0]
    row_at = lax.broadcasted_iota(jnp.int32, (size, size), 0)
    col_at = lax.broadcasted_iota(jnp.int32, (size, size), 1)
    hi, lo = split2(jnp.where(col_at <= row_at, work_ref[...], 0.0))
    copies = []
    for c in range(sample_ref.shape[1] // 256):
        at = pl.ds(c * 256, 256)
        sample = sample_ref[:, at]
        basis_v[:, at] = dot32(hi, sample) + dot32(lo, sample)
        copies.append(
            pltpu.make_async_copy(basis_v.at[:, at], basis_hbm.at[:, at], sems.at[c])
        )
        copies[-1].start()
    for copy in copies:
        copy.wait()


MESH = pl.DeviceIdType.MESH
ROWS_AXIS = 16
PROBE_AXIS = 8
RING = 4


def sample_kernel(
    ranks_ref,
    resp_hbm,
    probes_hbm,
    left_hbm,
    right_hbm,
    sample_out,
    gram_out,
    probes_v,
    right_v,
    left_v,
    resp_v,
    sample_v,
    sib_v,
    late_v,
    part_v,
    sum_v,
    near_v,
    near2_v,
    far_v,
    stage_v,
    last_v,
    local_sem,
    right_sem,
    near_send,
    near_recv,
    far_send,
    far_recv,
    sib_send,
    sib_recv,
    ring_send,
    ring_recv,
    forward_send,
    forward_recv,
    cross_send,
    cross_recv,
):
    r = lax.axis_index("rows")
    p = lax.axis_index("probe")
    core = r % 2
    high = (r // 2) % 2
    x = r // 4
    z = p // RING
    y = p % RING
    levels = right_v.shape[0]
    width = right_v.shape[1]
    local = probes_v.shape[0]
    pair_rows = resp_v.shape[2]
    half_rows = pair_rows // 2

    near = []
    for offset in (1, 2, 3):
        other = x * 4 + ((high + offset // 2) % 2) * 2 + (core + offset % 2) % 2
        near.append((other, p))
    in_plane = high * 2 + core
    x_pair = x + 1 - 2 * (x % 2)
    x_far = 2 - 2 * (x // 2)
    far = [(x_pair * 4 + in_plane, p), (x_far * 4 + in_plane, p), ((x_far + 1) * 4 + in_plane, p)]
    group = [(r, (p + d) % PROBE_AXIS) for d in range(1, PROBE_AXIS)]
    ring = [(r, z * RING + (y + d) % RING) for d in range(1, RING)]
    across = (r, (1 - z) * RING + y)

    barrier = pltpu.get_barrier_semaphore()
    for peer in near + far + group:
        pl.semaphore_signal(barrier, inc=1, device_id=peer, device_id_type=MESH)

    probes_copy = pltpu.make_async_copy(probes_hbm, probes_v, local_sem.at[0])
    probes_copy.start()
    rights = [
        pltpu.make_async_copy(right_hbm.at[l], right_v.at[l], right_sem.at[l]) for l in range(levels)
    ]
    depth = 2
    rights[0].start()

    def pair_columns(pair):
        return pl.ds(pl.multiple_of(pair * pair_rows, pair_rows), pair_rows)

    own_pair = y // 2
    own_rows = pl.ds(pl.multiple_of(p * local, local), local)
    across_rows = pl.ds(pl.multiple_of(across[1] * local, local), local)
    own_columns = pair_columns(p // 2)
    own_resp = pltpu.make_async_copy(
        resp_hbm.at[:, own_columns], resp_v.at[own_pair, own_rows, :], local_sem.at[1]
    )
    left_copy = pltpu.make_async_copy(left_hbm.at[:, :, own_columns], left_v, local_sem.at[2])

    lane = lax.broadcasted_iota(jnp.int32, (local, width), 1)

    def coupling(l, start, size):
        value = lax.dot_general(
            probes_v[:, start : start + size],
            right_v[l, :, start : start + size],
            (((1,), (1,)), ((), ())),
            preferred_element_type=jnp.float32,
        )
        return jnp.where(lane < ranks_ref[l], value, 0.0)

    def send(source, target, send_sem, recv_sem, peer):
        copy = pltpu.make_async_remote_copy(
            src_ref=source,
            dst_ref=target,
            send_sem=send_sem,
            recv_sem=recv_sem,
            device_id=peer,
            device_id_type=MESH,
        )
        copy.start()
        return copy

    def ready(l):
        rights[l].wait()
        if l == 0:
            rights[1].start()
        if l + depth < levels:
            rights[l + depth].start()
        elif l + depth == levels:
            own_resp.start()
            left_copy.start()

    def cross(i):
        half = i % 2
        pair = (own_pair + 1 + i // 2) % 2
        columns = pl.ds(
            pl.multiple_of(((1 - z) * 2 + pair) * pair_rows + half * half_rows, half_rows), half_rows
        )
        return send(
            resp_hbm.at[:, columns],
            resp_v.at[pair, own_rows, pl.ds(half * half_rows, half_rows)],
            cross_send.at[i],
            cross_recv.at[i],
            across,
        )

    total = probes_v.shape[1]
    probes_copy.wait()
    ready(0)
    part_v[0] = coupling(0, 0, total)
    pl.semaphore_wait(barrier, len(near) + len(far) + len(group))

    near_copies = [
        send(part_v.at[0], near_v.at[i], near_send.at[0, i], near_recv.at[0, i], near[i])
        for i in range(3)
    ]
    crossing = [cross(0)]
    ring_copies = []
    for d in (1, 0, 2):
        peer = ring[d]
        pair = (peer[1] % RING) // 2
        ring_copies.append(
            send(
                resp_hbm.at[:, pair_columns(peer[1] // 2)],
                resp_v.at[pair, own_rows, :],
                ring_send.at[0, d],
                ring_recv.at[0, d],
                peer,
            )
        )
    ready(1)
    part_v[1] = coupling(1, 0, total)
    near2_copies = [
        send(part_v.at[1], near2_v.at[i, 0], near_send.at[1, i], near_recv.at[1, i], near[i])
        for i in range(3)
    ]
    crossing.append(cross(1))
    ready(2)
    part_v[2] = coupling(2, 0, total)
    near3_copies = [
        send(part_v.at[2], near2_v.at[i, 1], near_send.at[2, i], near_recv.at[2, i], near[i])
        for i in (1, 2)
    ]
    crossing += [cross(2), cross(3)]
    ready(3)
    last_v[0] = coupling(3, 0, total).astype(jnp.bfloat16)
    core_copy = send(last_v.at[0], last_v.at[1], near_send.at[2, 0], near_recv.at[2, 0], near[0])
    ready(4)
    for c in range(2):
        stage_v[1 - c, :, 2 * width : 3 * width] = coupling(
            4, c * (total // 2), total // 2
        ).astype(jnp.bfloat16)

    forwards = []

    def forward_other(half):
        crossing[half].wait_recv()
        place = pl.ds(half * half_rows, half_rows)
        other = (own_pair + 1) % 2
        for member in range(2):
            peer = (r, z * RING + other * 2 + (y + member) % 2)
            forwards.append(
                pltpu.make_async_remote_copy(
                    src_ref=resp_v.at[other, across_rows, place],
                    dst_ref=resp_v.at[other, across_rows, place],
                    send_sem=forward_send.at[half, member],
                    recv_sem=forward_recv.at[half, y % 2],
                    device_id=peer,
                    device_id_type=MESH,
                )
            )
            forwards[-1].start()

    def forward_own(half):
        crossing[2 + half].wait_recv()
        place = pl.ds(half * half_rows, half_rows)
        peer = (r, p + 1 - 2 * (y % 2))
        forwards.append(
            send(
                resp_v.at[own_pair, across_rows, place],
                resp_v.at[own_pair, across_rows, place],
                forward_send.at[half, 2],
                forward_recv.at[half, 2],
                peer,
            )
        )

    forward_other(0)
    for copy in near_copies:
        copy.wait_recv()
    sum_v[0] = (part_v[0] + near_v[0]) + (near_v[1] + near_v[2])
    far_copies = [
        send(sum_v.at[0], far_v.at[x % 2], far_send.at[i], far_recv.at[x % 2], far[1 + i])
        for i in range(2)
    ]
    forward_other(1)
    for copy in near2_copies:
        copy.wait_recv()
    sum_v[1] = (part_v[1] + near2_v[0, 0]) + (near2_v[1, 0] + near2_v[2, 0])
    pair_copy = send(sum_v.at[1], far_v.at[2], far_send.at[2], far_recv.at[2], far[0])
    forward_own(0)
    core_copy.wait_recv()
    for copy in near3_copies:
        copy.wait_recv()
    level3 = (near2_v[1, 1] + near2_v[2, 1]).astype(jnp.bfloat16)
    for c in range(2):
        stage_v[c, :, :width] = level3
        stage_v[c, :, width : 2 * width] = last_v[1]

    def columns_of(first, count):
        return pl.ds(first * width, count * width)

    gathers = [
        send(
            stage_v.at[peer[1] // RING],
            sib_v.at[own_rows, columns_of(2, 3)],
            sib_send.at[0, d],
            sib_recv.at[0, d],
            peer,
        )
        for d, peer in enumerate(group)
    ]
    sib_v[own_rows, columns_of(2, 3)] = stage_v[z]

    forward_own(1)
    pair_copy.wait_recv()
    sib_v[own_rows, columns_of(1, 1)] = far_v[2].astype(jnp.bfloat16)
    for i in range(2):
        pltpu.make_async_remote_copy(
            src_ref=sum_v.at[0],
            dst_ref=far_v.at[i],
            send_sem=far_send.at[i],
            recv_sem=far_recv.at[i],
            device_id=far[1],
            device_id_type=MESH,
        ).wait_recv()
    sib_v[own_rows, columns_of(0, 1)] = (far_v[0] + far_v[1]).astype(jnp.bfloat16)
    gathers += [
        send(
            sib_v.at[own_rows, columns_of(0, 2)],
            sib_v.at[own_rows, columns_of(0, 2)],
            sib_send.at[1, d],
            sib_recv.at[1, d],
            peer,
        )
        for d, peer in enumerate(group)
    ]

    own_resp.wait()
    left_copy.wait()
    for copy in gathers[: len(group)]:
        copy.wait_recv()
    chunk = 512

    def update_of(first, count, at):
        siblings = sib_v[:, first * width : (first + count) * width]
        factors = left_v[first : first + count, :, at].reshape(count * width, chunk)
        return dot32(siblings, factors)

    for c in range(pair_rows // chunk):
        at = slice(c * chunk, (c + 1) * chunk)
        late_v[:, at] = update_of(2, 3, at)
    for copy in ring_copies + gathers[len(group) :]:
        copy.wait_recv()
    for half in range(2):
        place = pl.ds(half * half_rows, half_rows)
        for member in range(3):
            pltpu.make_async_remote_copy(
                src_ref=resp_v.at[own_pair, across_rows, place],
                dst_ref=resp_v.at[own_pair, across_rows, place],
                send_sem=forward_send.at[half, member],
                recv_sem=forward_recv.at[half, member],
                device_id=across,
                device_id_type=MESH,
            ).wait_recv()

    for c in range(pair_rows // chunk):
        at = slice(c * chunk, (c + 1) * chunk)
        update = update_of(0, 2, at) + late_v[:, at]
        sample_v[:, at] = (resp_v[own_pair, :, at].astype(jnp.float32) - update).astype(jnp.bfloat16)
    gram = lax.dot_general(
        sample_v[...],
        sample_v[...],
        (((1,), (1,)), ((), ())),
        preferred_element_type=jnp.float32,
    )
    size = gram.shape[0]
    row_at = lax.broadcasted_iota(jnp.int32, (size, size), 0)
    col_at = lax.broadcasted_iota(jnp.int32, (size, size), 1)
    gram_out[...] = gram + jnp.where(row_at == col_at, ridge_share * pair_rows, 0.0)
    half_at = pl.multiple_of((p % 2) * half_rows, half_rows)
    sample_out[...] = sample_v[:, pl.ds(half_at, half_rows)]

    sent = near_copies + near2_copies + near3_copies + [core_copy] + far_copies + [pair_copy]
    for copy in sent + ring_copies + crossing + forwards + gathers:
        copy.wait_send()


def shards(responses, probes, left_factors, right_factors, level_ranks):
    levels, width, rows_dev = right_factors.shape
    local = probes.shape[0]
    probe_count = local * PROBE_AXIS
    block_rows = rows_dev * ROWS_AXIS // BLOCKS
    slab_rows = rows_dev // PROBE_AXIS
    vmem = pl.BlockSpec(memory_space=pltpu.VMEM)
    anywhere = pl.BlockSpec(memory_space=pl.ANY)
    bf16, f32 = jnp.bfloat16, jnp.float32
    dma = pltpu.SemaphoreType.DMA
    sample, gram = pl.pallas_call(
        sample_kernel,
        out_shape=(
            jax.ShapeDtypeStruct((probe_count, slab_rows), bf16),
            jax.ShapeDtypeStruct((probe_count, probe_count), f32),
        ),
        in_specs=[pl.BlockSpec(memory_space=pltpu.SMEM)] + [anywhere] * 4,
        out_specs=(vmem, vmem),
        scratch_shapes=[
            pltpu.VMEM((local, rows_dev), bf16),
            pltpu.VMEM((levels, width, rows_dev), bf16),
            pltpu.VMEM((levels, width, block_rows), bf16),
            pltpu.VMEM((2, probe_count, block_rows), bf16),
            pltpu.VMEM((probe_count, block_rows), bf16),
            pltpu.VMEM((probe_count, levels * width), bf16),
            pltpu.VMEM((probe_count, block_rows), f32),
            pltpu.VMEM((3, local, width), f32),
            pltpu.VMEM((2, local, width), f32),
            pltpu.VMEM((3, local, width), f32),
            pltpu.VMEM((3, 2, local, width), f32),
            pltpu.VMEM((3, local, width), f32),
            pltpu.VMEM((2, local, 3 * width), bf16),
            pltpu.VMEM((2, local, width), bf16),
            dma((3,)),
            dma((levels,)),
            dma((3, 3)),
            dma((3, 3)),
            dma((3,)),
            dma((3,)),
            dma((2, PROBE_AXIS - 1)),
            dma((2, PROBE_AXIS - 1)),
            dma((1, RING - 1)),
            dma((1, RING - 1)),
            dma((2, 3)),
            dma((2, 3)),
            dma((4,)),
            dma((4,)),
        ],
        compiler_params=pltpu.CompilerParams(collective_id=0, has_side_effects=True),
        name="sample_and_gram",
    )(level_ranks, responses, probes, left_factors, right_factors)
    return pl.pallas_call(
        orthonormalize,
        out_shape=jax.ShapeDtypeStruct(sample.shape, f32),
        in_specs=[vmem] * 2,
        out_specs=anywhere,
        scratch_shapes=[
            pltpu.VMEM((probe_count, probe_count), f32),
            pltpu.VMEM(sample.shape, f32),
            dma((sample.shape[1] // 256,)),
        ],
        compiler_params=pltpu.CompilerParams(

        ),
        name="orthonormalize",
    )(gram, sample)


def solution(mesh):
    return jax.shard_map(
        shards,
        mesh=mesh,
        in_specs=(
            P("probe", "rows"),
            P("probe", "rows"),
            P(None, None, "rows"),
            P(None, None, "rows"),
            P(),
        ),
        out_specs=P(None, ("rows", "probe")),
        check_vma=False,
    )
```

```python
import jax
import jax.numpy as jnp
from jax import lax
from jax.experimental import pallas as pl
from jax.experimental.pallas import tpu as pltpu
from jax.sharding import PartitionSpec as P

BLOCKS = 64


ridge_share = 0.05


PANEL = 16


def split2(x):
    hi = x.astype(jnp.bfloat16)
    return hi, (x - hi.astype(jnp.float32)).astype(jnp.bfloat16)


def split3(x):
    hi = x.astype(jnp.bfloat16)
    rest = x - hi.astype(jnp.float32)
    mid = rest.astype(jnp.bfloat16)
    return hi, mid, (rest - mid.astype(jnp.float32)).astype(jnp.bfloat16)


def dot32(a, b):
    return jnp.dot(a, b, preferred_element_type=jnp.float32)


def invert_factor(t_ref):
    size = t_ref.shape[0]
    m = PANEL
    sub = lax.broadcasted_iota(jnp.int32, (8, 128), 0)
    lane = lax.broadcasted_iota(jnp.int32, (8, 128), 1)
    halves = range(size // 128)
    groups = range(m // 8)

    def spread(value, k):
        return jnp.broadcast_to(value[k : k + 1, :], (8, 128))

    for p in range(size // m):
        j0 = p * m
        g, jl = j0 // 128, j0 % 128
        panel = [
            [t_ref[pl.ds(j0 + 8 * q, 8), pl.ds(128 * h, 128)] for q in groups] for h in halves
        ]
        cols = [
            [jnp.broadcast_to(panel[g][q][:, jl + j : jl + j + 1], (8, 128)) for q in groups]
            for j in range(m)
        ]
        inside = (lane >= jl) & (lane < jl + m)
        for q in groups:
            identity = jnp.where(lane - jl - 8 * q == sub, 1.0, 0.0)
            panel[g][q] = jnp.where(inside, identity, panel[g][q])
        outs = [[] for _ in halves]
        for k in range(m):
            at, row = k // 8, k % 8
            pivot = spread(cols[k][at], row)
            inverse = 1.0 / pivot
            root = lax.rsqrt(pivot)
            here = sub == row
            factor = [cols[k][q] * inverse for q in groups]
            factor[at] = jnp.where(here, -inverse, factor[at])
            for j in range(k + 1, m):
                line = spread(cols[j][at], row)
                for q in groups:
                    base = jnp.where(here, 0.0, cols[j][q]) if q == at else cols[j][q]
                    if j == k + 1:
                        lead = jnp.where(here, -1.0, cols[k][q]) if q == at else cols[k][q]
                        cols[j][q] = base - (lead * line) * inverse
                    else:
                        cols[j][q] = base - factor[q] * line
            for h in halves:
                line = spread(panel[h][at], row)
                outs[h].append((line * root)[:1])
                for q in groups:
                    base = jnp.where(here, 0.0, panel[h][q]) if q == at else panel[h][q]
                    panel[h][q] = base - factor[q] * line
        for h in halves:
            t_ref[pl.ds(j0, m), pl.ds(128 * h, 128)] = jnp.concatenate(outs[h], 0)
        left = size - j0 - m
        if left:
            rest = pl.ds(j0 + m, left)
            lh, lm, ll = split3(t_ref[rest, pl.ds(128 * g, 128)][:, jl : jl + m])
            zh, zm, zl = split3(
                jnp.concatenate([jnp.concatenate(panel[h], 0) for h in halves], 1)
            )
            update = dot32(
                jnp.concatenate([lh, lm, ll, lh, lm, lh], 1),
                jnp.concatenate([zh, zh, zh, zm, zm, zl], 0),
            )
            at = lax.broadcasted_iota(jnp.int32, (left, size), 1)
            t_ref[rest, :] = jnp.where((at >= j0) & (at < j0 + m), 0.0, t_ref[rest, :]) - update


def orthonormalize(gram_ref, sample_ref, basis_hbm, work_ref, basis_v, sems):
    work_ref[...] = gram_ref[...]
    invert_factor(work_ref)
    size = work_ref.shape[0]
    row_at = lax.broadcasted_iota(jnp.int32, (size, size), 0)
    col_at = lax.broadcasted_iota(jnp.int32, (size, size), 1)
    hi, lo = split2(jnp.where(col_at <= row_at, work_ref[...], 0.0))
    copies = []
    for c in range(sample_ref.shape[1] // 256):
        at = pl.ds(c * 256, 256)
        sample = sample_ref[:, at]
        basis_v[:, at] = dot32(hi, sample) + dot32(lo, sample)
        copies.append(
            pltpu.make_async_copy(basis_v.at[:, at], basis_hbm.at[:, at], sems.at[c])
        )
        copies[-1].start()
    for copy in copies:
        copy.wait()


MESH = pl.DeviceIdType.MESH
ROWS_AXIS = 16
PROBE_AXIS = 8
RING = 4


def sample_kernel(
    ranks_ref,
    resp_hbm,
    probes_hbm,
    left_hbm,
    right_hbm,
    sample_out,
    gram_out,
    probes_v,
    resp_own_v,
    right_v,
    left_v,
    resp_v,
    sample_v,
    sib_v,
    late_v,
    part_v,
    sum_v,
    near_v,
    near2_v,
    far_v,
    stage_v,
    last_v,
    local_sem,
    right_sem,
    near_send,
    near_recv,
    far_send,
    far_recv,
    sib_send,
    sib_recv,
    ring_send,
    ring_recv,
    forward_send,
    forward_recv,
    cross_send,
    cross_recv,
):
    r = lax.axis_index("rows")
    p = lax.axis_index("probe")
    core = r % 2
    high = (r // 2) % 2
    x = r // 4
    z = p // RING
    y = p % RING
    levels = right_v.shape[0]
    width = right_v.shape[1]
    local = probes_v.shape[0]
    pair_rows = resp_v.shape[2]
    half_rows = pair_rows // 2

    near = []
    for offset in (1, 2, 3):
        other = x * 4 + ((high + offset // 2) % 2) * 2 + (core + offset % 2) % 2
        near.append((other, p))
    in_plane = high * 2 + core
    x_pair = x + 1 - 2 * (x % 2)
    x_far = 2 - 2 * (x // 2)
    far = [(x_pair * 4 + in_plane, p), (x_far * 4 + in_plane, p), ((x_far + 1) * 4 + in_plane, p)]
    group = [(r, (p + d) % PROBE_AXIS) for d in range(1, PROBE_AXIS)]
    ring = [(r, z * RING + (y + d) % RING) for d in range(1, RING)]
    across = (r, (1 - z) * RING + y)

    barrier = pltpu.get_barrier_semaphore()
    for peer in near + far + group:
        pl.semaphore_signal(barrier, inc=1, device_id=peer, device_id_type=MESH)

    probes_copy = pltpu.make_async_copy(probes_hbm, probes_v, local_sem.at[0])
    probes_copy.start()
    rights = [
        pltpu.make_async_copy(right_hbm.at[l], right_v.at[l], right_sem.at[l]) for l in range(levels)
    ]
    depth = 2
    rights[0].start()
    resp_copy = pltpu.make_async_copy(resp_hbm, resp_own_v, local_sem.at[3])
    resp_copy.start()

    def pair_columns(pair):
        return pl.ds(pl.multiple_of(pair * pair_rows, pair_rows), pair_rows)

    own_pair = y // 2
    own_rows = pl.ds(pl.multiple_of(p * local, local), local)
    across_rows = pl.ds(pl.multiple_of(across[1] * local, local), local)
    own_columns = pair_columns(p // 2)
    own_resp = pltpu.make_async_copy(
        resp_hbm.at[:, own_columns], resp_v.at[own_pair, own_rows, :], local_sem.at[1]
    )
    left_copy = pltpu.make_async_copy(left_hbm.at[:, :, own_columns], left_v, local_sem.at[2])

    lane = lax.broadcasted_iota(jnp.int32, (local, width), 1)

    def coupling(l, start, size):
        value = lax.dot_general(
            probes_v[:, start : start + size],
            right_v[l, :, start : start + size],
            (((1,), (1,)), ((), ())),
            preferred_element_type=jnp.float32,
        )
        return jnp.where(lane < ranks_ref[l], value, 0.0)

    def send(source, target, send_sem, recv_sem, peer):
        copy = pltpu.make_async_remote_copy(
            src_ref=source,
            dst_ref=target,
            send_sem=send_sem,
            recv_sem=recv_sem,
            device_id=peer,
            device_id_type=MESH,
        )
        copy.start()
        return copy

    def ready(l):
        rights[l].wait()
        if l == 0:
            rights[1].start()
        if l + depth < levels:
            rights[l + depth].start()
        elif l + depth == levels:
            own_resp.start()
            left_copy.start()

    def cross(i):
        half = i % 2
        pair = (own_pair + 1 + i // 2) % 2
        columns = pl.ds(
            pl.multiple_of(((1 - z) * 2 + pair) * pair_rows + half * half_rows, half_rows), half_rows
        )
        return send(
            resp_own_v.at[:, columns],
            resp_v.at[pair, own_rows, pl.ds(half * half_rows, half_rows)],
            cross_send.at[i],
            cross_recv.at[i],
            across,
        )

    total = probes_v.shape[1]
    probes_copy.wait()
    ready(0)
    part_v[0] = coupling(0, 0, total)
    pl.semaphore_wait(barrier, len(near) + len(far) + len(group))

    near_copies = [
        send(part_v.at[0], near_v.at[i], near_send.at[0, i], near_recv.at[0, i], near[i])
        for i in range(3)
    ]
    resp_copy.wait()
    crossing = [cross(0)]
    ring_copies = []
    for d in (1, 0, 2):
        peer = ring[d]
        pair = (peer[1] % RING) // 2
        ring_copies.append(
            send(
                resp_own_v.at[:, pair_columns(peer[1] // 2)],
                resp_v.at[pair, own_rows, :],
                ring_send.at[0, d],
                ring_recv.at[0, d],
                peer,
            )
        )
    ready(1)
    part_v[1] = coupling(1, 0, total)
    near2_copies = [
        send(part_v.at[1], near2_v.at[i, 0], near_send.at[1, i], near_recv.at[1, i], near[i])
        for i in range(3)
    ]
    crossing.append(cross(1))
    ready(2)
    part_v[2] = coupling(2, 0, total)
    near3_copies = [
        send(part_v.at[2], near2_v.at[i, 1], near_send.at[2, i], near_recv.at[2, i], near[i])
        for i in (1, 2)
    ]
    crossing += [cross(2), cross(3)]
    ready(3)
    last_v[0] = coupling(3, 0, total).astype(jnp.bfloat16)
    core_copy = send(last_v.at[0], last_v.at[1], near_send.at[2, 0], near_recv.at[2, 0], near[0])
    ready(4)
    for c in range(2):
        stage_v[1 - c, :, 2 * width : 3 * width] = coupling(
            4, c * (total // 2), total // 2
        ).astype(jnp.bfloat16)

    forwards = []

    def forward_other(half):
        crossing[half].wait_recv()
        place = pl.ds(half * half_rows, half_rows)
        other = (own_pair + 1) % 2
        for member in range(2):
            peer = (r, z * RING + other * 2 + (y + member) % 2)
            forwards.append(
                pltpu.make_async_remote_copy(
                    src_ref=resp_v.at[other, across_rows, place],
                    dst_ref=resp_v.at[other, across_rows, place],
                    send_sem=forward_send.at[half, member],
                    recv_sem=forward_recv.at[half, y % 2],
                    device_id=peer,
                    device_id_type=MESH,
                )
            )
            forwards[-1].start()

    def forward_own(half):
        crossing[2 + half].wait_recv()
        place = pl.ds(half * half_rows, half_rows)
        peer = (r, p + 1 - 2 * (y % 2))
        forwards.append(
            send(
                resp_v.at[own_pair, across_rows, place],
                resp_v.at[own_pair, across_rows, place],
                forward_send.at[half, 2],
                forward_recv.at[half, 2],
                peer,
            )
        )

    forward_other(0)
    forward_other(1)
    for copy in near_copies:
        copy.wait_recv()
    sum_v[0] = (part_v[0] + near_v[0]) + (near_v[1] + near_v[2])
    far_copies = [
        send(sum_v.at[0], far_v.at[x % 2], far_send.at[i], far_recv.at[x % 2], far[1 + i])
        for i in range(2)
    ]
    for copy in near2_copies:
        copy.wait_recv()
    sum_v[1] = (part_v[1] + near2_v[0, 0]) + (near2_v[1, 0] + near2_v[2, 0])
    pair_copy = send(sum_v.at[1], far_v.at[2], far_send.at[2], far_recv.at[2], far[0])
    forward_own(0)
    core_copy.wait_recv()
    for copy in near3_copies:
        copy.wait_recv()
    level3 = (near2_v[1, 1] + near2_v[2, 1]).astype(jnp.bfloat16)
    for c in range(2):
        stage_v[c, :, :width] = level3
        stage_v[c, :, width : 2 * width] = last_v[1]

    def columns_of(first, count):
        return pl.ds(first * width, count * width)

    gathers = [
        send(
            stage_v.at[peer[1] // RING],
            sib_v.at[own_rows, columns_of(2, 3)],
            sib_send.at[0, d],
            sib_recv.at[0, d],
            peer,
        )
        for d, peer in enumerate(group)
    ]
    sib_v[own_rows, columns_of(2, 3)] = stage_v[z]

    forward_own(1)
    pair_copy.wait_recv()
    sib_v[own_rows, columns_of(1, 1)] = far_v[2].astype(jnp.bfloat16)
    for i in range(2):
        pltpu.make_async_remote_copy(
            src_ref=sum_v.at[0],
            dst_ref=far_v.at[i],
            send_sem=far_send.at[i],
            recv_sem=far_recv.at[i],
            device_id=far[1],
            device_id_type=MESH,
        ).wait_recv()
    sib_v[own_rows, columns_of(0, 1)] = (far_v[0] + far_v[1]).astype(jnp.bfloat16)
    gathers += [
        send(
            sib_v.at[own_rows, columns_of(0, 2)],
            sib_v.at[own_rows, columns_of(0, 2)],
            sib_send.at[1, d],
            sib_recv.at[1, d],
            peer,
        )
        for d, peer in enumerate(group)
    ]

    own_resp.wait()
    left_copy.wait()
    for copy in gathers[: len(group)]:
        copy.wait_recv()
    chunk = 512

    def update_of(first, count, at):
        siblings = sib_v[:, first * width : (first + count) * width]
        factors = left_v[first : first + count, :, at].reshape(count * width, chunk)
        return dot32(siblings, factors)

    for c in range(pair_rows // chunk):
        at = slice(c * chunk, (c + 1) * chunk)
        late_v[:, at] = update_of(2, 3, at)
    for copy in ring_copies + gathers[len(group) :]:
        copy.wait_recv()
    for half in range(2):
        place = pl.ds(half * half_rows, half_rows)
        for member in range(3):
            pltpu.make_async_remote_copy(
                src_ref=resp_v.at[own_pair, across_rows, place],
                dst_ref=resp_v.at[own_pair, across_rows, place],
                send_sem=forward_send.at[half, member],
                recv_sem=forward_recv.at[half, member],
                device_id=across,
                device_id_type=MESH,
            ).wait_recv()

    for c in range(pair_rows // chunk):
        at = slice(c * chunk, (c + 1) * chunk)
        update = update_of(0, 2, at) + late_v[:, at]
        sample_v[:, at] = (resp_v[own_pair, :, at].astype(jnp.float32) - update).astype(jnp.bfloat16)
    gram = lax.dot_general(
        sample_v[...],
        sample_v[...],
        (((1,), (1,)), ((), ())),
        preferred_element_type=jnp.float32,
    )
    size = gram.shape[0]
    row_at = lax.broadcasted_iota(jnp.int32, (size, size), 0)
    col_at = lax.broadcasted_iota(jnp.int32, (size, size), 1)
    gram_out[...] = gram + jnp.where(row_at == col_at, ridge_share * pair_rows, 0.0)
    half_at = pl.multiple_of((p % 2) * half_rows, half_rows)
    sample_out[...] = sample_v[:, pl.ds(half_at, half_rows)]

    sent = near_copies + near2_copies + near3_copies + [core_copy] + far_copies + [pair_copy]
    for copy in sent + ring_copies + crossing + forwards + gathers:
        copy.wait_send()


def shards(responses, probes, left_factors, right_factors, level_ranks):
    levels, width, rows_dev = right_factors.shape
    local = probes.shape[0]
    probe_count = local * PROBE_AXIS
    block_rows = rows_dev * ROWS_AXIS // BLOCKS
    slab_rows = rows_dev // PROBE_AXIS
    vmem = pl.BlockSpec(memory_space=pltpu.VMEM)
    anywhere = pl.BlockSpec(memory_space=pl.ANY)
    bf16, f32 = jnp.bfloat16, jnp.float32
    dma = pltpu.SemaphoreType.DMA
    sample, gram = pl.pallas_call(
        sample_kernel,
        out_shape=(
            jax.ShapeDtypeStruct((probe_count, slab_rows), bf16),
            jax.ShapeDtypeStruct((probe_count, probe_count), f32),
        ),
        in_specs=[pl.BlockSpec(memory_space=pltpu.SMEM)] + [anywhere] * 4,
        out_specs=(vmem, vmem),
        scratch_shapes=[
            pltpu.VMEM((local, rows_dev), bf16),
            pltpu.VMEM((local, rows_dev), bf16),
            pltpu.VMEM((levels, width, rows_dev), bf16),
            pltpu.VMEM((levels, width, block_rows), bf16),
            pltpu.VMEM((2, probe_count, block_rows), bf16),
            pltpu.VMEM((probe_count, block_rows), bf16),
            pltpu.VMEM((probe_count, levels * width), bf16),
            pltpu.VMEM((probe_count, block_rows), f32),
            pltpu.VMEM((3, local, width), f32),
            pltpu.VMEM((2, local, width), f32),
            pltpu.VMEM((3, local, width), f32),
            pltpu.VMEM((3, 2, local, width), f32),
            pltpu.VMEM((3, local, width), f32),
            pltpu.VMEM((2, local, 3 * width), bf16),
            pltpu.VMEM((2, local, width), bf16),
            dma((4,)),
            dma((levels,)),
            dma((3, 3)),
            dma((3, 3)),
            dma((3,)),
            dma((3,)),
            dma((2, PROBE_AXIS - 1)),
            dma((2, PROBE_AXIS - 1)),
            dma((1, RING - 1)),
            dma((1, RING - 1)),
            dma((2, 3)),
            dma((2, 3)),
            dma((4,)),
            dma((4,)),
        ],
        compiler_params=pltpu.CompilerParams(collective_id=0, has_side_effects=True),
        name="sample_and_gram",
    )(level_ranks, responses, probes, left_factors, right_factors)
    return pl.pallas_call(
        orthonormalize,
        out_shape=jax.ShapeDtypeStruct(sample.shape, f32),
        in_specs=[vmem] * 2,
        out_specs=anywhere,
        scratch_shapes=[
            pltpu.VMEM((probe_count, probe_count), f32),
            pltpu.VMEM(sample.shape, f32),
            dma((sample.shape[1] // 256,)),
        ],
        compiler_params=pltpu.CompilerParams(

        ),
        name="orthonormalize",
    )(gram, sample)


def solution(mesh):
    return jax.shard_map(
        shards,
        mesh=mesh,
        in_specs=(
            P("probe", "rows"),
            P("probe", "rows"),
            P(None, None, "rows"),
            P(None, None, "rows"),
            P(),
        ),
        out_specs=P(None, ("rows", "probe")),
        check_vma=False,
    )
```
